32 devices in a mesh: seg: 8 (over y, x, core), head: 4 (over z).
Axes of the slice: x: 2, y: 2, z: 4, core: 2. Of those that a mesh axis runs over, the one named last changes fastest.
Arguments:
- layer_input: bfloat16 [1, 4096, 2048], P(None, 'seg', 'head'), may hold values from -160 to 160, as said below
- w_qkv: bfloat16 [2048, 3, 1024], P(None, None, 'head'), may hold values from -3 to 3
- comp_weight: bfloat16 [3, 2, 1024], P(None, None, 'head'), may hold values from -2.5 to 2.5
- w_out: bfloat16 [1024, 2048], P('seg', 'head'), may hold values from -1.5 to 1.5
Outputs:
- attn_out: bfloat16 [1, 4096, 2048], P(None, 'seg', 'head')
The draws below stay inside these ranges and needn't reach their ends.
Inputs may be any that keep to these rules, and one draw needn't show every extreme that they name: layer_input varies in scale from feature to feature and from token to token.
All inputs are finite; a program needn't handle non-finite values.
Results may differ from the reference program's by a relative error of at most 0.0089.
Values may be sent and summed in bfloat16 or wider, within the bound.
No kernel may reach another device: no remote copies, remote signals or barrier semaphores. Data moves between devices by JAX's collectives and lax.ppermute only.
A program may use at most 64 MiB of HBM per device.

```python
import math
import jax
import jax.numpy as jnp
from jax import lax

D = 2048
HEADS = 8
DH = 128
SEG_LEN = 512
BOOKS = 1
HD = 1024
TOKENS = 4096
N_SEG = 8


def draw_layer_input(key, part):
    key_col, key_row, key_base = jax.random.split(key, 3)
    shape = (BOOKS, TOKENS, D)
    col_scale = jnp.exp(jax.random.uniform(key_col, (D,), jnp.float32, 0.0, math.log(10.0)))
    row_scale = jnp.exp(jax.random.uniform(key_row, (BOOKS, TOKENS, 1), jnp.float32, 0.0, math.log(4.0)))
    base = jax.random.truncated_normal(key_base, -4.0, 4.0, shape, jnp.float32)
    return jnp.clip(base * col_scale * row_scale, -160.0, 160.0).astype(jnp.bfloat16)


def draw_w_qkv(key, part):
    key_base = jax.random.fold_in(key, 0)
    base = jax.random.truncated_normal(key_base, -4.0, 4.0, (D, 3, HD), jnp.float32) / math.sqrt(D)
    return jnp.clip(base, -3.0, 3.0).astype(jnp.bfloat16)


def shard_levels(stream_key, extent, pieces, least, top_value):
    gain = 1.0
    for dim, blocks in pieces:
        draws = jax.random.uniform(jax.random.fold_in(jax.random.fold_in(stream_key, 6), dim), (blocks,), jnp.float32, least / len(pieces), top_value / len(pieces))
        gain = gain * jnp.repeat(jnp.exp(draws), extent[dim] // blocks).reshape((-1,) + (1,) * (len(extent) - 1 - dim))
    return gain


def scatter_about(own_key, shape, deviation, limit, cuts=(), kind=jnp.bfloat16):
    values = jax.random.normal(own_key, shape, jnp.float32) * deviation
    if len(cuts) > 0:
        values = shard_levels(own_key, shape, cuts, -0.22, 0.18) * values
    return jnp.clip(values, min=-limit, max=limit).astype(kind)


def setup_inputs(seed: int = 0) -> dict:
    seeds = jax.random.split(jax.random.key(seed), 5)
    layer_input = draw_layer_input(jax.random.fold_in(seeds[4], 71), 0)
    w_qkv = draw_w_qkv(jax.random.fold_in(seeds[4], 71), 0)
    comp_weight = scatter_about(seeds[2], (3, 2, HD), 0.6, 2.5, ((2, 4),))
    w_out = scatter_about(seeds[3], (HD, D), (HD // 64) ** -0.5, 1.5, ((0, 8), (1, 4)))
    return dict(layer_input=layer_input, w_qkv=w_qkv, comp_weight=comp_weight, w_out=w_out)


def layer_norm(values):
    center_mean = lax.optimization_barrier(jnp.mean(values, axis=-1, keepdims=True))
    centered = values - center_mean
    variance = lax.optimization_barrier(jnp.mean(centered * centered, axis=-1, keepdims=True))
    return centered * lax.rsqrt(variance + 1e-05)

def compress(source, weight):
    grouped = source.astype(jnp.float32).reshape(2, SEG_LEN, 3, HD)
    return jnp.einsum('kltc,tkc->klc', grouped, weight.astype(jnp.float32)).astype(jnp.bfloat16)

def key_allowed(segment):
    query_pos = jnp.arange(SEG_LEN)[:, None]
    key_pos = jnp.arange(3 * SEG_LEN)[None, :]
    own_part = (key_pos >= 2 * SEG_LEN) & (key_pos - 2 * SEG_LEN <= query_pos)
    memory_part = (key_pos >= SEG_LEN) & (key_pos < 2 * SEG_LEN) & (segment >= 1)
    comp_part = (key_pos < SEG_LEN) & (segment >= 4)
    return own_part | memory_part | comp_part

def attend(queries, keyed, valued, segment):
    query_heads = queries.astype(jnp.float32).reshape(SEG_LEN, HEADS, DH)
    key_heads = keyed.astype(jnp.float32).reshape(3 * SEG_LEN, HEADS, DH)
    value_heads = valued.astype(jnp.float32).reshape(3 * SEG_LEN, HEADS, DH)
    scores = jnp.einsum('qhd,khd->hqk', query_heads, key_heads) / math.sqrt(DH)
    scores = jnp.where(key_allowed(segment)[None], scores, jnp.float32(-1e+30))
    highest = lax.optimization_barrier(jnp.max(scores, axis=-1, keepdims=True))
    exponent = jnp.exp(scores - highest)
    weights = (exponent / lax.optimization_barrier(jnp.sum(exponent, axis=-1, keepdims=True))).astype(jnp.bfloat16)
    mixed = jnp.einsum('hqk,khd->qhd', weights.astype(jnp.float32), value_heads)
    return mixed.astype(jnp.bfloat16).reshape(SEG_LEN, HD)

def reference(layer_input, w_qkv, comp_weight, w_out):

    def one_book(book_rows):
        normed = layer_norm(book_rows.astype(jnp.float32)).astype(jnp.bfloat16)
        projected = jnp.dot(normed, w_qkv.reshape(D, 3 * HD), preferred_element_type=jnp.float32)
        projected = projected.astype(jnp.bfloat16).reshape(TOKENS, 3, HD)
        queries = projected[:, 0]
        key_vals = jnp.moveaxis(projected[:, 1:3], 1, 0)
        padded = jnp.concatenate([jnp.zeros((2, 4 * SEG_LEN, HD), jnp.bfloat16), key_vals], axis=1)

        def one_segment(segment):
            offset = (segment * SEG_LEN).astype(jnp.int32)
            window = lax.dynamic_slice_in_dim(padded, offset, 5 * SEG_LEN, 1)
            compressed = compress(window[:, :3 * SEG_LEN], comp_weight)
            joined = jnp.concatenate([compressed, window[:, 3 * SEG_LEN:]], axis=1)
            seg_queries = lax.dynamic_slice_in_dim(queries, offset, SEG_LEN, 0)
            context = attend(seg_queries, joined[0], joined[1], segment)
            return jnp.dot(context, w_out, preferred_element_type=jnp.float32).astype(jnp.bfloat16)
        outputs = lax.map(one_segment, jnp.arange(N_SEG, dtype=jnp.int32))
        return outputs.reshape(TOKENS, D)
    return lax.map(one_book, layer_input)
```

```python
import math

import jax
import jax.numpy as jnp
from jax import lax
from jax.experimental import pallas as pl
from jax.experimental.pallas import tpu as pltpu
from jax.sharding import PartitionSpec as P


DH = 128
RATE = 3
BACK = 4
BF16 = jnp.bfloat16
F32 = jnp.float32
NEG = -1e30
VMEM_LIMIT = 48 * 1024 * 1024


def params():
    return pltpu.CompilerParams(vmem_limit_bytes=VMEM_LIMIT)


def vmem():
    return pl.BlockSpec(memory_space=pltpu.VMEM)


def smem():
    return pl.BlockSpec(memory_space=pltpu.SMEM)


def after(value, *deps):
    return lax.optimization_barrier((value,) + deps)[0]


def around(block, axis):
    size = lax.axis_size(axis)
    return lax.ppermute(block, axis, [(i, (i + 1) % size) for i in range(size)])


def passed_along(block, distance, first=0):
    size = lax.axis_size("seg")
    route = [(i - distance, i) for i in range(size) if i >= distance and i >= first]
    return lax.ppermute(block, "seg", route)


def project_kernel(n_head, n_chunk, place, *refs):
    blocks = refs[: n_head * n_chunk]
    w_ref, q_ref, kv_ref = refs[n_head * n_chunk :]
    z = place[1]
    rows, feats = blocks[0].shape
    width = w_ref.shape[2]
    total = n_head * feats
    for c in range(n_chunk):
        here = [blocks[c * n_head + t][...].astype(F32) for t in range(n_head)]
        mean = sum(jnp.sum(v, axis=1, keepdims=True) for v in here) / total
        here = [v - mean for v in here]
        var = sum(jnp.sum(v * v, axis=1, keepdims=True) for v in here) / total
        inv = lax.rsqrt(var + 1e-05)
        normed = [(v * inv).astype(BF16) for v in here]
        at = pl.ds(c * rows, rows)
        for i in range(3):
            acc = jnp.zeros((rows, width), F32)
            for t in range(n_head):
                source = lax.rem(z - t + n_head, n_head)
                start = pl.multiple_of(source * feats, feats)
                acc += jnp.dot(
                    normed[t], w_ref[i, pl.ds(start, feats), :], preferred_element_type=F32
                )
            if i == 0:
                q_ref[at, :] = acc.astype(BF16)
            else:
                kv_ref[at, (i - 1) * width : i * width] = acc.astype(BF16)


def project(place, chunks, w3):
    n_head = len(chunks[0])
    flat = [b for chunk in chunks for b in chunk]
    rows = sum(chunk[0].shape[0] for chunk in chunks)
    width = w3.shape[2]
    return pl.pallas_call(
        lambda *refs: project_kernel(n_head, len(chunks), *refs),
        out_shape=(
            jax.ShapeDtypeStruct((rows, width), BF16),
            jax.ShapeDtypeStruct((rows, 2 * width), BF16),
        ),
        in_specs=[smem()] + [vmem()] * (len(flat) + 1),
        out_specs=(vmem(), vmem()),
        compiler_params=params(),
        name="project",
    )(place, *flat, w3)


class Slots:
    def __init__(self, seg_len, early_rows):
        self.offset = [(-a * seg_len) % RATE for a in range(RATE)]
        self.count = [(seg_len - o) // RATE for o in self.offset]
        self.tail = [seg_len - o - RATE * n for o, n in zip(self.offset, self.count)]
        self.early = [max(0, (early_rows - o) // RATE) for o in self.offset]
        self.late = [n - e for n, e in zip(self.count, self.early)]
        most = max(
            max(e + o for e, o in zip(self.early, self.offset)),
            max(l + t for l, t in zip(self.late, self.tail)),
        )
        self.rows = -(-most // 16) * 16
        self.joints = [b for b in range(RATE - 1) if self.tail[b] > 0]


def compress_kernel(slots, late, *refs):
    n_in = 2 if late else 1
    sources = refs[:n_in]
    w_ref = refs[n_in]
    outs = refs[n_in + 1 :]
    weight = w_ref[...].astype(F32)
    n = slots.rows
    starts = []
    seen = 0
    for s in sources:
        starts.append(seen)
        seen += s.shape[0]
    picked = {}

    def pick(first, step, count, shift):
        total = None
        for base, s in zip(starts, sources):
            row = lax.broadcasted_iota(jnp.int32, (n, s.shape[0]), 0)
            col = lax.broadcasted_iota(jnp.int32, (n, s.shape[0]), 1) + base
            hit = (col == first + step * (row - shift)) & (row >= shift) & (row < shift + count)
            one = jnp.where(hit, 1.0, 0.0).astype(BF16)
            part = jnp.dot(one, s[...], preferred_element_type=F32)
            total = part if total is None else total + part
        return total

    for a in range(RATE):
        begin = slots.early[a] if late else 0
        count = slots.late[a] if late else slots.early[a]
        acc = None
        for r in range(RATE):
            first = slots.offset[a] + RATE * begin + r
            key = (first, count)
            if key not in picked:
                picked[key] = pick(first, RATE, count, 0)
            term = picked[key] * weight[r : r + 1, :]
            acc = term if acc is None else acc + term
        raw_rows = slots.tail[a] if late else slots.offset[a]
        if raw_rows:
            first = seen - raw_rows if late else 0
            acc = acc + pick(first, 1, raw_rows, count)
        outs[a][...] = acc.astype(BF16)


def compress(slots, late, sources, weight):
    width = weight.shape[1]
    return pl.pallas_call(
        lambda *refs: compress_kernel(slots, late, *refs),
        out_shape=tuple(jax.ShapeDtypeStruct((slots.rows, width), BF16) for _ in range(RATE)),
        in_specs=[vmem()] * (len(sources) + 1),
        out_specs=tuple(vmem() for _ in range(RATE)),
        compiler_params=params(),
        name="compress",
    )(*sources, weight)


def attend_kernel(slots, n_own, place, q_ref, *refs):
    own = refs[:n_own]
    memory = refs[n_own : n_own + 2]
    early = refs[n_own + 2 : n_own + 2 + RATE]
    late = refs[n_own + 2 + RATE : n_own + 2 + 2 * RATE]
    w_ref, out_ref, comp_ref = refs[n_own + 2 + 2 * RATE :]
    seg = place[0]
    rows, width = q_ref.shape
    n = slots.rows
    weight = w_ref[...].astype(F32)
    n_comp = comp_ref.shape[0]
    for a in range(RATE):
        comp_ref[a * n : (a + 1) * n, :] = early[a][...]
        comp_ref[(RATE + a) * n : (RATE + a + 1) * n, :] = late[a][...]
    pad = n_comp - 2 * RATE * n
    row = lax.broadcasted_iota(jnp.int32, (pad, 2 * width), 0)
    extra = jnp.zeros((pad, 2 * width), F32)
    for k, b in enumerate(slots.joints):
        at = slots.late[b]
        tail = late[b][...].astype(F32)
        head = early[b + 1][...].astype(F32)
        parts = [tail[at + i : at + i + 1] for i in range(slots.tail[b])]
        at = slots.early[b + 1]
        parts += [head[at + i : at + i + 1] for i in range(slots.offset[b + 1])]
        slot = sum(p * weight[r : r + 1] for r, p in enumerate(parts))
        extra = jnp.where(row == k, slot, extra)
    comp_ref[2 * RATE * n :, :] = extra.astype(BF16)

    col = lax.broadcasted_iota(jnp.int32, (1, n_comp), 1)
    valid = col < 0
    for a in range(RATE):
        valid |= (col >= a * n) & (col < a * n + slots.early[a])
        valid |= (col >= (RATE + a) * n) & (col < (RATE + a) * n + slots.late[a])
    valid |= (col >= 2 * RATE * n) & (col < 2 * RATE * n + len(slots.joints))
    valid &= seg >= BACK
    comp_bias = jnp.where(valid, 0.0, NEG)
    mem_bias = jnp.where(seg >= 1, 0.0, NEG).astype(F32)
    scale = 1.0 / math.sqrt(DH) * math.log2(math.e)
    q_row = lax.broadcasted_iota(jnp.int32, (rows, rows), 0)
    k_row = lax.broadcasted_iota(jnp.int32, (rows, rows), 1)
    causal = k_row <= q_row
    for h in range(width // DH):
        kc = slice(h * DH, (h + 1) * DH)
        vc = slice(width + h * DH, width + (h + 1) * DH)
        q = q_ref[:, kc]

        def score(keys):
            return lax.dot_general(
                q, keys, (((1,), (1,)), ((), ())), preferred_element_type=F32
            )

        pieces = [(score(comp_ref[:, kc]) + comp_bias, comp_ref[:, vc])]
        for m in memory:
            pieces.append((score(m[:, kc]) + mem_bias, m[:, vc]))
        for o in own[:-1]:
            pieces.append((score(o[:, kc]), o[:, vc]))
        pieces.append((jnp.where(causal, score(own[-1][:, kc]), NEG), own[-1][:, vc]))
        top = None
        for s, _ in pieces:
            m = jnp.max(s, axis=1, keepdims=True)
            top = m if top is None else jnp.maximum(top, m)
        norm = jnp.zeros((rows, 1), F32)
        mixed = jnp.zeros((rows, DH), F32)
        for s, v in pieces:
            p = jnp.exp2((s - top) * scale)
            norm += jnp.sum(p, axis=1, keepdims=True)
            mixed += jnp.dot(p.astype(BF16), v, preferred_element_type=F32)
        out_ref[:, kc] = (mixed / norm).astype(BF16)


def attend(slots, place, q, own, memory, early, late, weight):
    rows, width = q.shape
    n_comp = -(-(2 * RATE * slots.rows + 16) // 128) * 128
    args = [q, *own, *memory, *early, *late, weight]
    return pl.pallas_call(
        lambda *refs: attend_kernel(slots, len(own), *refs),
        out_shape=jax.ShapeDtypeStruct((rows, width), BF16),
        in_specs=[smem()] + [vmem()] * len(args),
        out_specs=vmem(),
        scratch_shapes=[pltpu.VMEM((n_comp, 2 * width), BF16)],
        compiler_params=params(),
        name="attend",
    )(place, *args)


def output_kernel(n_head, place, *refs):
    ctx = refs[:n_head]
    w_ref, _, out_ref = refs[n_head:]
    z = place[1]
    width = ctx[0].shape[1]
    acc = None
    for t in range(n_head):
        source = lax.rem(z - t + n_head, n_head)
        start = pl.multiple_of(source * width, width)
        part = jnp.dot(ctx[t][...], w_ref[pl.ds(start, width), :], preferred_element_type=F32)
        acc = part if acc is None else acc + part
    out_ref[...] = acc.astype(BF16)


def output(place, half, n_half, ctx, w_full, result):
    rows, width = ctx[0].shape
    columns = w_full.shape[1]
    n_head = len(ctx)
    whole = jax.ShapeDtypeStruct((rows * n_half, columns), BF16)

    def body(place, *refs):
        if result is None:
            refs = refs[:-1] + (None, refs[-1])
        output_kernel(n_head, place, *refs)

    args = [place, *ctx, w_full]
    full = lambda a: pl.BlockSpec(a.shape, lambda i: (0,) * a.ndim)
    in_specs = [smem()] + [full(a) for a in args[1:]]
    aliases = {}
    if result is not None:
        args.append(result)
        in_specs.append(pl.BlockSpec(memory_space=pl.ANY))
        aliases = {len(args) - 1: 0}
    return pl.pallas_call(
        body,
        grid=(1,),
        out_shape=whole,
        in_specs=in_specs,
        out_specs=pl.BlockSpec((rows, columns), lambda i: (half, 0)),
        input_output_aliases=aliases,
        compiler_params=params(),
        name="output",
    )(*args)


def gather_rows(block):
    size = lax.axis_size("seg")
    if size & (size - 1):
        return lax.all_gather(block, "seg", axis=0, tiled=True)
    seg = lax.axis_index("seg")
    step = 1
    while step < size:
        other = lax.ppermute(block, "seg", [(i, i ^ step) for i in range(size)])
        upper = (seg // step) % 2 == 1
        low = jnp.where(upper, other, block)
        high = jnp.where(upper, block, other)
        block = jnp.concatenate([low, high], axis=0)
        step *= 2
    return block


def local(layer_input, w_qkv, comp_weight, w_out):
    n_head = lax.axis_size("head")
    seg_len = layer_input.shape[1]
    rows = layer_input[0]
    w3 = jnp.transpose(w_qkv, (1, 0, 2))
    width = w_qkv.shape[2]
    weight = comp_weight.reshape(RATE, 2 * width)
    place = jnp.stack([lax.axis_index("seg"), lax.axis_index("head")]).astype(jnp.int32)

    n_chunk, n_half = 4, 2
    per_half = n_chunk // n_half
    piece = seg_len // n_chunk
    half_rows = seg_len // n_half
    slots = Slots(seg_len, half_rows)

    halves = []
    dep = None
    for h in range(n_half):
        chunks = []
        for c in range(per_half):
            at = (h * per_half + c) * piece
            mine = lax.slice_in_dim(rows, at, at + piece, axis=0)
            if dep is not None:
                mine = after(mine, dep)
            chunks.append([mine])
        for t in range(1, n_head):
            for c in range(per_half):
                chunks[c].append(around(chunks[c][-1], "head"))
        dep = chunks[0][-2]
        halves.append(chunks)

    w_full = gather_rows(w_out)

    qs, kvs, mems, comps = [], [], [], []
    for h in range(n_half):
        q, kv = project(place, halves[h], w3)
        qs.append(q)
        kvs.append(kv)
        mems.append(passed_along(kv, 1))
        parts = compress(slots, h == 1, kvs[: h + 1], weight)
        comps.append([passed_along(p, BACK - a, BACK) for a, p in enumerate(parts)])

    result = None
    rings = []
    for h in range(n_half):
        ctx = attend(slots, place, qs[h], kvs[: h + 1], mems, comps[0], comps[1], weight)
        rings.append([ctx])
    for t in range(1, n_head):
        for ring in rings:
            ring.append(around(ring[-1], "head"))
    for h, ring in enumerate(rings):
        result = output(place, h, n_half, ring, w_full, result)
    return result[None]


def solution(mesh):
    return jax.shard_map(
        local,
        mesh=mesh,
        in_specs=(
            P(None, "seg", "head"),
            P(None, None, "head"),
            P(None, None, "head"),
            P("seg", "head"),
        ),
        out_specs=P(None, "seg", "head"),
        check_vma=False,
    )
```

```python
import math

import jax
import jax.numpy as jnp
from jax import lax
from jax.experimental import pallas as pl
from jax.experimental.pallas import tpu as pltpu
from jax.sharding import PartitionSpec as P


DH = 128
RATE = 3
BACK = 4
BF16 = jnp.bfloat16
F32 = jnp.float32
NEG = -1e30
VMEM_LIMIT = 14 * 1024 * 1024


def params():
    return pltpu.CompilerParams(vmem_limit_bytes=VMEM_LIMIT)


def vmem():
    return pl.BlockSpec(memory_space=pltpu.VMEM)


def smem():
    return pl.BlockSpec(memory_space=pltpu.SMEM)


def after(value, *deps):
    return lax.optimization_barrier((value,) + deps)[0]


def ring_order(size):
    ups = [i for i in range(size) if i % 2 == 1]
    downs = [i for i in range(size) if i % 2 == 0 and i > 0]
    return [0] + ups + downs[::-1]


def around(block, axis):
    order = ring_order(lax.axis_size(axis))
    route = [(a, b) for a, b in zip(order, order[1:] + order[:1])]
    return lax.ppermute(block, axis, route)


def passed_along(block, distance, first=0):
    size = lax.axis_size("seg")
    route = [(i - distance, i) for i in range(size) if i >= distance and i >= first]
    return lax.ppermute(block, "seg", route)


def whereabouts():
    size = lax.axis_size("head")
    order = ring_order(size)
    table = [
        [order[(order.index(z) - t) % size] for t in range(size)] for z in range(size)
    ]
    mine = jnp.asarray(table, jnp.int32)[lax.axis_index("head")]
    seg = lax.axis_index("seg").astype(jnp.int32)
    return jnp.concatenate([seg[None], mine])


def call(body, outs, args, name, scratch=()):
    return pl.pallas_call(
        body,
        out_shape=tuple(jax.ShapeDtypeStruct(s, d) for s, d in outs),
        in_specs=[smem()] + [vmem()] * (len(args) - 1),
        out_specs=tuple(vmem() for _ in outs),
        scratch_shapes=list(scratch),
        compiler_params=params(),
        name=name,
    )(*args)


def weight_rows(w_ref, i, source, feats):
    start = pl.multiple_of(source * feats, feats)
    return w_ref[i, pl.ds(start, feats), :]


def moments(block):
    x = block.astype(F32)
    total = jnp.sum(x, axis=1, keepdims=True)
    off = x - total / x.shape[1]
    return total, jnp.sum(off * off, axis=1, keepdims=True)


def joined_moments(parts, feats):
    count = feats * len(parts)
    mean = sum(t for t, _ in parts) / count
    square = sum(q + feats * jnp.square(t / feats - mean) for t, q in parts)
    return mean, lax.rsqrt(square / count + 1e-05)


def project_sum(place, blocks, steps, w_ref, i):
    feats = blocks[0].shape[1]
    acc = None
    for t, block in zip(steps, blocks):
        part = jnp.dot(
            block[...], weight_rows(w_ref, i, place[1 + t], feats), preferred_element_type=F32
        )
        acc = part if acc is None else acc + part
    return acc


def project(place, chunks, w3):
    n_head, n_chunk = len(chunks[0]), len(chunks)
    piece, feats = chunks[0][0].shape
    width = w3.shape[2]
    rows = piece * n_chunk

    def body(place, *refs):
        w_ref, q_ref, kv_ref, sum_ref = refs[n_head * n_chunk :]
        col_sums = [jnp.sum(w_ref[i].astype(F32), axis=0, keepdims=True) for i in range(3)]
        for i in range(3):
            sum_ref[:, i * width : (i + 1) * width] = jnp.broadcast_to(col_sums[i], (8, width))
        for c in range(n_chunk):
            blocks = refs[c * n_head : (c + 1) * n_head]
            mean, inv = joined_moments([moments(b[...]) for b in blocks], feats)
            at = pl.ds(c * piece, piece)
            for i in range(3):
                acc = project_sum(place, blocks, range(n_head), w_ref, i)
                acc = ((acc - mean * col_sums[i]) * inv).astype(BF16)
                if i == 0:
                    q_ref[at, :] = acc
                else:
                    kv_ref[at, (i - 1) * width : i * width] = acc

    flat = [b for chunk in chunks for b in chunk]
    outs = [((rows, width), BF16), ((rows, 2 * width), BF16), ((8, 3 * width), F32)]
    return call(body, outs, [place, *flat, w3], "project")


def project_begin(place, chunks, w3):
    n_here, n_chunk = len(chunks[0]), len(chunks)
    piece, feats = chunks[0][0].shape
    width = w3.shape[2]

    def body(place, *refs):
        w_ref, acc_ref, mom_ref = refs[n_here * n_chunk :]
        lane = lax.broadcasted_iota(jnp.int32, (piece, 128), 1)
        for c in range(n_chunk):
            blocks = refs[c * n_here : (c + 1) * n_here]
            at = pl.ds(c * piece, piece)
            for i in range(3):
                acc_ref[at, i * width : (i + 1) * width] = project_sum(
                    place, blocks, range(n_here), w_ref, i
                )
            held = jnp.zeros((piece, 128), F32)
            for t, block in enumerate(blocks):
                for k, value in enumerate(moments(block[...])):
                    held = jnp.where(lane == 2 * t + k, value, held)
            mom_ref[at, :] = held

    flat = [b for chunk in chunks for b in chunk]
    outs = [((piece * n_chunk, 3 * width), F32), ((piece * n_chunk, 128), F32)]
    return call(body, outs, [place, *flat, w3], "project_begin")


def project_end(slots, place, lasts, begun, w3, col_sums, before, weight):
    n_chunk = len(lasts)
    piece, feats = lasts[0].shape
    width = w3.shape[2]
    rows = piece * n_chunk
    n_head = w3.shape[1] // feats
    last = n_head - 1

    def body(place, *refs):
        w_ref, acc_ref, mom_ref, sum_ref, before_ref, cw_ref = refs[n_chunk : n_chunk + 6]
        q_ref, kv_ref, *outs = refs[n_chunk + 6 :]
        for c in range(n_chunk):
            at = pl.ds(c * piece, piece)
            held = mom_ref[at, :]
            parts = [(held[:, 2 * t : 2 * t + 1], held[:, 2 * t + 1 : 2 * t + 2]) for t in range(last)]
            parts.append(moments(refs[c][...]))
            mean, inv = joined_moments(parts, feats)
            for i in range(3):
                cols = slice(i * width, (i + 1) * width)
                acc = acc_ref[at, cols] + project_sum(place, [refs[c]], [last], w_ref, i)
                acc = ((acc - mean * sum_ref[0:1, cols]) * inv).astype(BF16)
                if i == 0:
                    q_ref[at, :] = acc
                else:
                    kv_ref[at, (i - 1) * width : i * width] = acc
        write_slots(slots, True, [before_ref, kv_ref], cw_ref, outs)

    outs = [((rows, width), BF16), ((rows, 2 * width), BF16)]
    outs += [((slots.rows, 2 * width), BF16)] * RATE
    args = [place, *lasts, w3, *begun, col_sums, before, weight]
    return call(body, outs, args, "project_end")


class Slots:
    def __init__(self, seg_len, early_rows):
        self.seg_len, self.early_rows = seg_len, early_rows
        self.offset = [(-a * seg_len) % RATE for a in range(RATE)]
        self.count = [(seg_len - o) // RATE for o in self.offset]
        self.tail = [seg_len - o - RATE * n for o, n in zip(self.offset, self.count)]
        self.early = [max(0, (early_rows - o) // RATE) for o in self.offset]
        self.late = [n - e for n, e in zip(self.count, self.early)]
        most = max(
            max(e + o for e, o in zip(self.early, self.offset)),
            max(l + t for l, t in zip(self.late, self.tail)),
        )
        self.rows = -(-most // 16) * 16
        self.joints = [b for b in range(RATE - 1) if self.tail[b] > 0]


def write_slots(slots, late, sources, w_ref, outs):
    weight = w_ref[...].astype(F32)
    n = slots.rows
    main = sources[-1]
    base = slots.early_rows if late else 0
    counts = slots.late if late else slots.early
    begins = slots.early if late else [0] * RATE
    firsts = [slots.offset[a] + RATE * begins[a] for a in range(RATE)]
    wanted = sorted({f + r for f in firsts for r in range(RATE)})

    def hits(first, rows, at):
        row = lax.broadcasted_iota(jnp.int32, (n, rows), 0)
        col = lax.broadcasted_iota(jnp.int32, (n, rows), 1) + at
        return jnp.where(col == first + RATE * row, 1.0, 0.0).astype(BF16)

    chosen = jnp.concatenate([hits(f, main.shape[0], base) for f in wanted], axis=0)
    picks = jnp.dot(chosen, main[...], preferred_element_type=F32)
    row = lax.broadcasted_iota(jnp.int32, (n, 1), 0)
    picked = {}
    for k, f in enumerate(wanted):
        got = picks[k * n : (k + 1) * n]
        if f < base:
            back = base - f
            got = jnp.where(row == 0, sources[0][-16:, :].astype(F32)[16 - back : 17 - back], got)
        picked[f] = got
    raw = main[...].astype(F32)
    for a in range(RATE):
        acc = None
        for r in range(RATE):
            term = picked[firsts[a] + r] * weight[r : r + 1, :]
            acc = term if acc is None else acc + term
        n_raw = slots.tail[a] if late else slots.offset[a]
        for i in range(n_raw):
            at = main.shape[0] - n_raw + i if late else i
            acc = jnp.where(row == counts[a] + i, raw[at : at + 1, :], acc)
        outs[a][...] = acc.astype(BF16)


def compress_early(slots, place, source, weight):
    def body(place, source_ref, w_ref, *outs):
        write_slots(slots, False, [source_ref], w_ref, outs)

    outs = [((slots.rows, weight.shape[1]), BF16)] * RATE
    return call(body, outs, [place, source, weight], "compress")


SCALE = math.log2(math.e) / math.sqrt(DH)


def score(q, keys):
    return lax.dot_general(q, keys, (((1,), (1,)), ((), ())), preferred_element_type=F32)


def slot_bias(seg, n_cols, spans):
    col = lax.broadcasted_iota(jnp.int32, (1, n_cols), 1)
    valid = col < 0
    for begin, count in spans:
        valid |= (col >= begin) & (col < begin + count)
    return jnp.where(valid & (seg >= BACK), 0.0, NEG).astype(F32)


def attend_begin(slots, place, q, own, memory, early):
    rows, width = q.shape
    n = slots.rows
    n_comp = -(-RATE * n // 128) * 128
    heads = width // DH

    def body(place, q_ref, *refs):
        own_refs = refs[: len(own)]
        mem_ref = refs[len(own)]
        early_refs = refs[len(own) + 1 : len(own) + 1 + RATE]
        mix_ref, stat_ref, comp_ref = refs[len(own) + 1 + RATE :]
        seg = place[0]
        for a in range(RATE):
            comp_ref[a * n : (a + 1) * n, :] = early_refs[a][...]
        if n_comp > RATE * n:
            comp_ref[RATE * n :, :] = jnp.zeros((n_comp - RATE * n, 2 * width), BF16)
        comp_bias = slot_bias(seg, n_comp, [(a * n, slots.early[a]) for a in range(RATE)])
        mem_bias = jnp.where(seg >= 1, 0.0, NEG).astype(F32)
        q_row = lax.broadcasted_iota(jnp.int32, (rows, rows), 0)
        k_row = lax.broadcasted_iota(jnp.int32, (rows, rows), 1)
        causal = k_row <= q_row
        lane = lax.broadcasted_iota(jnp.int32, (rows, 128), 1)
        stats = jnp.zeros((rows, 128), F32)
        for h in range(heads):
            kc = slice(h * DH, (h + 1) * DH)
            vc = slice(width + h * DH, width + (h + 1) * DH)
            q = q_ref[:, kc]
            pieces = [
                (score(q, comp_ref[:, kc]) + comp_bias, comp_ref, vc),
                (score(q, mem_ref[:, kc]) + mem_bias, mem_ref, vc),
            ]
            for o in own_refs[:-1]:
                pieces.append((score(q, o[:, kc]), o, vc))
            o = own_refs[-1]
            pieces.append((jnp.where(causal, score(q, o[:, kc]), NEG), o, vc))
            top, norm, mixed = gathered(pieces, None)
            mix_ref[:, kc] = mixed
            stats = jnp.where(lane == 2 * h, top, stats)
            stats = jnp.where(lane == 2 * h + 1, norm, stats)
        stat_ref[...] = stats

    outs = [((rows, width), F32), ((rows, 128), F32)]
    scratch = [pltpu.VMEM((n_comp, 2 * width), BF16)]
    return call(body, outs, [place, q, *own, memory, *early], "attend_begin", scratch)


def gathered(pieces, so_far):
    top = None if so_far is None else so_far[0]
    for s, _, _ in pieces:
        m = jnp.max(s, axis=1, keepdims=True)
        top = m if top is None else jnp.maximum(top, m)
    norm = mixed = None
    if so_far is not None:
        shrink = jnp.exp2((so_far[0] - top) * SCALE)
        norm, mixed = so_far[1] * shrink, so_far[2] * shrink
    for s, v, cols in pieces:
        p = jnp.exp2((s - top) * SCALE)
        total = jnp.sum(p, axis=1, keepdims=True)
        part = jnp.dot(p.astype(BF16), v[:, cols], preferred_element_type=F32)
        norm = total if norm is None else norm + total
        mixed = part if mixed is None else mixed + part
    return top, norm, mixed


def attend_end(slots, place, q, begun, memory, heads_of, late, weight):
    rows, width = q.shape
    n = slots.rows
    n_comp = -(-(RATE * n + 16) // 128) * 128
    heads = width // DH

    def body(place, q_ref, mix_ref, stat_ref, mem_ref, *refs):
        early_refs = refs[:RATE]
        late_refs = refs[RATE : 2 * RATE]
        w_ref, out_ref, comp_ref = refs[2 * RATE :]
        seg = place[0]
        weight = w_ref[...].astype(F32)
        for a in range(RATE):
            comp_ref[a * n : (a + 1) * n, :] = late_refs[a][...]
        pad = n_comp - RATE * n
        row = lax.broadcasted_iota(jnp.int32, (pad, 1), 0)
        extra = jnp.zeros((pad, 2 * width), F32)
        for k, b in enumerate(slots.joints):
            at = slots.late[b]
            tail = late_refs[b][...].astype(F32)
            parts = [tail[at + i : at + i + 1] for i in range(slots.tail[b])]
            at = slots.early[b + 1]
            head = early_refs[b + 1][...].astype(F32)
            parts += [head[at + i : at + i + 1] for i in range(slots.offset[b + 1])]
            slot = sum(p * weight[r : r + 1] for r, p in enumerate(parts))
            extra = jnp.where(row == k, slot, extra)
        comp_ref[RATE * n :, :] = extra.astype(BF16)
        spans = [(a * n, slots.late[a]) for a in range(RATE)] + [(RATE * n, len(slots.joints))]
        comp_bias = slot_bias(seg, n_comp, spans)
        mem_bias = jnp.where(seg >= 1, 0.0, NEG).astype(F32)
        for h in range(heads):
            kc = slice(h * DH, (h + 1) * DH)
            vc = slice(width + h * DH, width + (h + 1) * DH)
            q = q_ref[:, kc]
            pieces = [
                (score(q, comp_ref[:, kc]) + comp_bias, comp_ref, vc),
                (score(q, mem_ref[:, kc]) + mem_bias, mem_ref, vc),
            ]
            so_far = (
                stat_ref[:, 2 * h : 2 * h + 1],
                stat_ref[:, 2 * h + 1 : 2 * h + 2],
                mix_ref[:, kc],
            )
            top, norm, mixed = gathered(pieces, so_far)
            out_ref[:, kc] = (mixed / norm).astype(BF16)

    outs = [((rows, width), BF16)]
    scratch = [pltpu.VMEM((n_comp, 2 * width), BF16)]
    args = [place, q, *begun, memory, *heads_of, *late, weight]
    return call(body, outs, args, "attend_end", scratch)[0]


def output_part(place, ctx, steps, w_ref):
    width = ctx[0].shape[1]
    acc = None
    for t, c in zip(steps, ctx):
        start = pl.multiple_of(place[1 + t] * width, width)
        part = jnp.dot(c[...], w_ref[pl.ds(start, width), :], preferred_element_type=F32)
        acc = part if acc is None else acc + part
    return acc


def output_begin(place, ctx, w_full):
    rows = ctx[0].shape[0]

    def body(place, *refs):
        w_ref, acc_ref = refs[len(ctx) :]
        acc_ref[...] = output_part(place, refs[: len(ctx)], range(len(ctx)), w_ref)

    outs = [((rows, w_full.shape[1]), F32)]
    return call(body, outs, [place, *ctx, w_full], "output_begin")[0]


def output_end(place, half, n_half, last_step, ctx, begun, w_full, result):
    rows = ctx.shape[0]
    columns = w_full.shape[1]
    n_in = 5 if result is not None else 4

    def body(place, ctx_ref, acc_ref, w_ref, *refs):
        out_ref, held, sem = refs[n_in - 4 :]
        acc = acc_ref[...] + output_part(place, [ctx_ref], [last_step], w_ref)
        held[...] = acc.astype(BF16)
        copy = pltpu.make_async_copy(held, out_ref.at[pl.ds(half * rows, rows), :], sem)
        copy.start()
        copy.wait()

    args = [place, ctx, begun, w_full]
    in_specs = [smem(), vmem(), vmem(), vmem()]
    aliases = {}
    if result is not None:
        args.append(result)
        in_specs.append(pl.BlockSpec(memory_space=pl.ANY))
        aliases = {4: 0}
    return pl.pallas_call(
        body,
        out_shape=jax.ShapeDtypeStruct((rows * n_half, columns), BF16),
        in_specs=in_specs,
        out_specs=pl.BlockSpec(memory_space=pl.ANY),
        scratch_shapes=[pltpu.VMEM((rows, columns), BF16), pltpu.SemaphoreType.DMA],
        input_output_aliases=aliases,
        compiler_params=params(),
        name="output_end",
    )(*args)


def gather_rows(block):
    size = lax.axis_size("seg")
    if size & (size - 1):
        return lax.all_gather(block, "seg", axis=0, tiled=True)
    seg = lax.axis_index("seg")
    step = 1
    while step < size:
        other = lax.ppermute(block, "seg", [(i, i ^ step) for i in range(size)])
        upper = (seg // step) % 2 == 1
        low = jnp.where(upper, other, block)
        high = jnp.where(upper, block, other)
        block = jnp.concatenate([low, high], axis=0)
        step *= 2
    return block


def local(layer_input, w_qkv, comp_weight, w_out):
    n_head = lax.axis_size("head")
    seg_len = layer_input.shape[1]
    rows = layer_input[0]
    w3 = jnp.transpose(w_qkv, (1, 0, 2))
    width = w_qkv.shape[2]
    weight = comp_weight.reshape(RATE, 2 * width)
    place = whereabouts()

    n_chunk, n_half = 4, 2
    per_half = n_chunk // n_half
    piece = seg_len // n_chunk
    half_rows = seg_len // n_half
    slots = Slots(seg_len, half_rows)

    def pieces(source, half):
        starts = [(half * per_half + c) * piece for c in range(per_half)]
        return [[lax.slice_in_dim(source, at, at + piece, axis=0)] for at in starts]

    first = pieces(rows, 0)
    for t in range(1, n_head):
        for chunk in first:
            chunk.append(around(chunk[-1], "head"))
    w_full = gather_rows(w_out)
    q0, kv0, col_sums = project(place, first, w3)
    early_parts = compress_early(slots, place, kv0, weight)
    mem0 = passed_along(kv0, 1)
    early = [passed_along(p, BACK - a, BACK) for a, p in enumerate(early_parts)]

    second = pieces(after(rows, first[0][-2]), 1)
    for t in range(1, n_head):
        for c, chunk in enumerate(second):
            block = chunk[-1]
            if t == 2 and c == 0:
                block = after(block, kv0)
            if t == 3 and c == 0:
                block = after(block, *early_parts)
            chunk.append(around(block, "head"))
    begun = project_begin(place, [chunk[:-1] for chunk in second], w3)
    lasts = [chunk[-1] for chunk in second]
    q1, kv1, *late = project_end(slots, place, lasts, begun, w3, col_sums, kv0, weight)
    mem1 = passed_along(kv1, 1)
    late = [passed_along(p, BACK - a, BACK) for a, p in enumerate(late)]

    rings = []
    for q, own in ((q0, [kv0]), (q1, [kv0, kv1])):
        part = attend_begin(slots, place, q, own, mem0, early)
        rings.append([attend_end(slots, place, q, part, mem1, early, late, weight)])
    for t in range(1, n_head):
        for ring in rings:
            ring.append(around(ring[-1], "head"))
    result = None
    for h, ring in enumerate(rings):
        part = output_begin(place, ring[:-1], w_full)
        result = output_end(place, h, n_half, n_head - 1, ring[-1], part, w_full, result)
    return result[None]


def solution(mesh):
    return jax.shard_map(
        local,
        mesh=mesh,
        in_specs=(
            P(None, "seg", "head"),
            P(None, None, "head"),
            P(None, None, "head"),
            P("seg", "head"),
        ),
        out_specs=P(None, "seg", "head"),
        check_vma=False,
    )
```

```python
import math

import jax
import jax.numpy as jnp
from jax import lax
from jax.experimental import pallas as pl
from jax.experimental.pallas import tpu as pltpu
from jax.sharding import PartitionSpec as P


DH = 128
RATE = 3
BACK = 4
BF16 = jnp.bfloat16
F32 = jnp.float32
NEG = -1e30
VMEM_LIMIT = 14 * 1024 * 1024


def params():
    return pltpu.CompilerParams(vmem_limit_bytes=VMEM_LIMIT)


def vmem():
    return pl.BlockSpec(memory_space=pltpu.VMEM)


def smem():
    return pl.BlockSpec(memory_space=pltpu.SMEM)


def after(value, *deps):
    return lax.optimization_barrier((value,) + deps)[0]


def ring_order(size):
    ups = [i for i in range(size) if i % 2 == 1]
    downs = [i for i in range(size) if i % 2 == 0 and i > 0]
    return [0] + ups + downs[::-1]


def around(block):
    order = ring_order(lax.axis_size("head"))
    route = [(a, b) for a, b in zip(order, order[1:] + order[:1])]
    return lax.ppermute(block, "head", route)


def passed_along(block, distance):
    size = lax.axis_size("seg")
    route = [(i, (i + distance) % size) for i in range(size)]
    return lax.ppermute(block, "seg", route)


def whereabouts():
    size = lax.axis_size("head")
    order = ring_order(size)
    table = [
        [order[(order.index(z) - t) % size] for t in range(size)] for z in range(size)
    ]
    mine = jnp.asarray(table, jnp.int32)[lax.axis_index("head")]
    seg = lax.axis_index("seg").astype(jnp.int32)
    return jnp.concatenate([seg[None], mine])


def call(body, outs, args, scratch=()):
    return pl.pallas_call(
        body,
        out_shape=tuple(jax.ShapeDtypeStruct(s, d) for s, d in outs),
        in_specs=[smem()] + [vmem()] * (len(args) - 1),
        out_specs=tuple(vmem() for _ in outs),
        scratch_shapes=list(scratch),
        compiler_params=params(),
    )(*args)


def weight_rows(w_ref, i, source, feats):
    start = pl.multiple_of(source * feats, feats)
    return w_ref[i, pl.ds(start, feats), :]


def moments(block):
    x = block.astype(F32)
    total = jnp.sum(x, axis=1, keepdims=True)
    off = x - total / x.shape[1]
    return total, jnp.sum(off * off, axis=1, keepdims=True)


def joined_moments(parts, feats):
    count = feats * len(parts)
    mean = sum(t for t, _ in parts) / count
    square = sum(q + feats * jnp.square(t / feats - mean) for t, q in parts)
    return mean, lax.rsqrt(square / count + 1e-05)


def project_sum(place, blocks, steps, w_ref, i):
    feats = blocks[0].shape[1]
    acc = None
    for t, block in zip(steps, blocks):
        part = jnp.dot(
            block[...], weight_rows(w_ref, i, place[1 + t], feats), preferred_element_type=F32
        )
        acc = part if acc is None else acc + part
    return acc


def fetch_weights(w3):
    n_kind, _, width = w3.shape

    def body(src, w_ref, sum_ref, sems):
        copies = [
            pltpu.make_async_copy(src.at[i], w_ref.at[i], sems.at[i]) for i in range(n_kind)
        ]
        for copy in copies:
            copy.start()
        for i, copy in enumerate(copies):
            copy.wait()
            total = jnp.sum(w_ref[i].astype(F32), axis=0, keepdims=True)
            sum_ref[:, i * width : (i + 1) * width] = jnp.broadcast_to(total, (8, width))

    return pl.pallas_call(
        body,
        out_shape=(
            jax.ShapeDtypeStruct(w3.shape, w3.dtype),
            jax.ShapeDtypeStruct((8, n_kind * width), F32),
        ),
        in_specs=[pl.BlockSpec(memory_space=pl.ANY)],
        out_specs=(vmem(), vmem()),
        scratch_shapes=[pltpu.SemaphoreType.DMA((n_kind,))],
        compiler_params=params(),
        name="fetch",
    )(w3)


def project(place, chunks, w3, col_sums):
    n_head, n_chunk = len(chunks[0]), len(chunks)
    piece, feats = chunks[0][0].shape
    width = w3.shape[2]
    rows = piece * n_chunk

    def body(place, *refs):
        w_ref, sum_ref, q_ref, kv_ref = refs[n_head * n_chunk :]
        for c in range(n_chunk):
            blocks = refs[c * n_head : (c + 1) * n_head]
            mean, inv = joined_moments([moments(b[...]) for b in blocks], feats)
            at = pl.ds(c * piece, piece)
            for i in range(3):
                acc = project_sum(place, blocks, range(n_head), w_ref, i)
                cols = slice(i * width, (i + 1) * width)
                acc = ((acc - mean * sum_ref[0:1, cols]) * inv).astype(BF16)
                if i == 0:
                    q_ref[at, :] = acc
                else:
                    kv_ref[at, (i - 1) * width : i * width] = acc

    flat = [b for chunk in chunks for b in chunk]
    outs = [((rows, width), BF16), ((rows, 2 * width), BF16)]
    return call(body, outs, [place, *flat, w3, col_sums])


def project_begin(place, chunks, w3):
    n_here, n_chunk = len(chunks[0]), len(chunks)
    piece, _ = chunks[0][0].shape
    width = w3.shape[2]

    def body(place, *refs):
        w_ref, acc_ref, mom_ref = refs[n_here * n_chunk :]
        lane = lax.broadcasted_iota(jnp.int32, (piece, 128), 1)
        for c in range(n_chunk):
            blocks = refs[c * n_here : (c + 1) * n_here]
            at = pl.ds(c * piece, piece)
            for i in range(3):
                acc_ref[at, i * width : (i + 1) * width] = project_sum(
                    place, blocks, range(n_here), w_ref, i
                )
            held = jnp.zeros((piece, 128), F32)
            for t, block in enumerate(blocks):
                for k, value in enumerate(moments(block[...])):
                    held = jnp.where(lane == 2 * t + k, value, held)
            mom_ref[at, :] = held

    flat = [b for chunk in chunks for b in chunk]
    outs = [((piece * n_chunk, 3 * width), F32), ((piece * n_chunk, 128), F32)]
    return call(body, outs, [place, *flat, w3])


def project_end(slots, place, lasts, begun, w3, col_sums, before, weight):
    n_chunk = len(lasts)
    piece, feats = lasts[0].shape
    width = w3.shape[2]
    rows = piece * n_chunk
    n_head = w3.shape[1] // feats
    last = n_head - 1

    def body(place, *refs):
        w_ref, acc_ref, mom_ref, sum_ref, before_ref, cw_ref = refs[n_chunk : n_chunk + 6]
        q_ref, kv_ref, *outs = refs[n_chunk + 6 :]
        for c in range(n_chunk):
            at = pl.ds(c * piece, piece)
            held = mom_ref[at, :]
            parts = [(held[:, 2 * t : 2 * t + 1], held[:, 2 * t + 1 : 2 * t + 2]) for t in range(last)]
            parts.append(moments(refs[c][...]))
            mean, inv = joined_moments(parts, feats)
            for i in range(3):
                cols = slice(i * width, (i + 1) * width)
                acc = acc_ref[at, cols] + project_sum(place, [refs[c]], [last], w_ref, i)
                acc = ((acc - mean * sum_ref[0:1, cols]) * inv).astype(BF16)
                if i == 0:
                    q_ref[at, :] = acc
                else:
                    kv_ref[at, (i - 1) * width : i * width] = acc
        write_slots(slots, True, [before_ref, kv_ref], cw_ref, outs)

    outs = [((rows, width), BF16), ((rows, 2 * width), BF16)]
    outs += [((slots.rows, 2 * width), BF16)] * RATE
    args = [place, *lasts, w3, *begun, col_sums, before, weight]
    return call(body, outs, args)


class Slots:
    def __init__(self, seg_len, early_rows):
        self.seg_len, self.early_rows = seg_len, early_rows
        self.offset = [(-a * seg_len) % RATE for a in range(RATE)]
        self.count = [(seg_len - o) // RATE for o in self.offset]
        self.tail = [seg_len - o - RATE * n for o, n in zip(self.offset, self.count)]
        self.early = [max(0, (early_rows - o) // RATE) for o in self.offset]
        self.late = [n - e for n, e in zip(self.count, self.early)]
        most = max(
            max(e + o for e, o in zip(self.early, self.offset)),
            max(l + t for l, t in zip(self.late, self.tail)),
        )
        self.rows = -(-most // 16) * 16
        self.joints = [b for b in range(RATE - 1) if self.tail[b] > 0]


def write_slots(slots, late, sources, w_ref, outs):
    weight = w_ref[...].astype(F32)
    n = slots.rows
    main = sources[-1]
    base = slots.early_rows if late else 0
    counts = slots.late if late else slots.early
    begins = slots.early if late else [0] * RATE
    firsts = [slots.offset[a] + RATE * begins[a] for a in range(RATE)]
    wanted = sorted({f + r for f in firsts for r in range(RATE)})

    def hits(first, rows, at):
        row = lax.broadcasted_iota(jnp.int32, (n, rows), 0)
        col = lax.broadcasted_iota(jnp.int32, (n, rows), 1) + at
        return jnp.where(col == first + RATE * row, 1.0, 0.0).astype(BF16)

    chosen = jnp.concatenate([hits(f, main.shape[0], base) for f in wanted], axis=0)
    picks = jnp.dot(chosen, main[...], preferred_element_type=F32)
    row = lax.broadcasted_iota(jnp.int32, (n, 1), 0)
    picked = {}
    for k, f in enumerate(wanted):
        got = picks[k * n : (k + 1) * n]
        if f < base:
            back = base - f
            got = jnp.where(row == 0, sources[0][-16:, :].astype(F32)[16 - back : 17 - back], got)
        picked[f] = got
    raw = main[...].astype(F32)
    for a in range(RATE):
        acc = None
        for r in range(RATE):
            term = picked[firsts[a] + r] * weight[r : r + 1, :]
            acc = term if acc is None else acc + term
        n_raw = slots.tail[a] if late else slots.offset[a]
        for i in range(n_raw):
            at = main.shape[0] - n_raw + i if late else i
            acc = jnp.where(row == counts[a] + i, raw[at : at + 1, :], acc)
        outs[a][...] = acc.astype(BF16)


def compress_early(slots, place, source, weight):
    def body(place, source_ref, w_ref, *outs):
        write_slots(slots, False, [source_ref], w_ref, outs)

    outs = [((slots.rows, weight.shape[1]), BF16)] * RATE
    return call(body, outs, [place, source, weight])


SCALE = math.log2(math.e) / math.sqrt(DH)


def score(q, keys):
    return lax.dot_general(q, keys, (((1,), (1,)), ((), ())), preferred_element_type=F32)


def slot_bias(seg, n_cols, spans):
    col = lax.broadcasted_iota(jnp.int32, (1, n_cols), 1)
    valid = col < 0
    for begin, count in spans:
        valid |= (col >= begin) & (col < begin + count)
    return jnp.where(valid & (seg >= BACK), 0.0, NEG).astype(F32)


def attend_begin(slots, place, q, own, memory, early):
    rows, width = q.shape
    n = slots.rows
    n_comp = -(-RATE * n // 128) * 128
    heads = width // DH

    def body(place, q_ref, *refs):
        own_refs = refs[: len(own)]
        mem_ref = refs[len(own)]
        early_refs = refs[len(own) + 1 : len(own) + 1 + RATE]
        mix_ref, stat_ref, comp_ref = refs[len(own) + 1 + RATE :]
        seg = place[0]
        for a in range(RATE):
            comp_ref[a * n : (a + 1) * n, :] = early_refs[a][...]
        if n_comp > RATE * n:
            comp_ref[RATE * n :, :] = jnp.zeros((n_comp - RATE * n, 2 * width), BF16)
        comp_bias = slot_bias(seg, n_comp, [(a * n, slots.early[a]) for a in range(RATE)])
        mem_bias = jnp.where(seg >= 1, 0.0, NEG).astype(F32)
        q_row = lax.broadcasted_iota(jnp.int32, (rows, rows), 0)
        k_row = lax.broadcasted_iota(jnp.int32, (rows, rows), 1)
        causal = k_row <= q_row
        lane = lax.broadcasted_iota(jnp.int32, (rows, 128), 1)
        stats = jnp.zeros((rows, 128), F32)
        for h in range(heads):
            kc = slice(h * DH, (h + 1) * DH)
            vc = slice(width + h * DH, width + (h + 1) * DH)
            q = q_ref[:, kc]
            pieces = [
                (score(q, comp_ref[:, kc]) + comp_bias, comp_ref, vc),
                (score(q, mem_ref[:, kc]) + mem_bias, mem_ref, vc),
            ]
            for o in own_refs[:-1]:
                pieces.append((score(q, o[:, kc]), o, vc))
            o = own_refs[-1]
            pieces.append((jnp.where(causal, score(q, o[:, kc]), NEG), o, vc))
            top, norm, mixed = gathered(pieces, None)
            mix_ref[:, kc] = mixed
            stats = jnp.where(lane == 2 * h, top, stats)
            stats = jnp.where(lane == 2 * h + 1, norm, stats)
        stat_ref[...] = stats

    outs = [((rows, width), F32), ((rows, 128), F32)]
    scratch = [pltpu.VMEM((n_comp, 2 * width), BF16)]
    return call(body, outs, [place, q, *own, memory, *early], scratch)


def gathered(pieces, so_far):
    top = None if so_far is None else so_far[0]
    for s, _, _ in pieces:
        m = jnp.max(s, axis=1, keepdims=True)
        top = m if top is None else jnp.maximum(top, m)
    norm = mixed = None
    if so_far is not None:
        shrink = jnp.exp2((so_far[0] - top) * SCALE)
        norm, mixed = so_far[1] * shrink, so_far[2] * shrink
    for s, v, cols in pieces:
        p = jnp.exp2((s - top) * SCALE)
        total = jnp.sum(p, axis=1, keepdims=True)
        part = jnp.dot(p.astype(BF16), v[:, cols], preferred_element_type=F32)
        norm = total if norm is None else norm + total
        mixed = part if mixed is None else mixed + part
    return top, norm, mixed


def attend_end(slots, place, q, begun, memory, heads_of, late, weight):
    rows, width = q.shape
    n = slots.rows
    n_comp = -(-(RATE * n + 16) // 128) * 128
    heads = width // DH

    def body(place, q_ref, mix_ref, stat_ref, mem_ref, *refs):
        early_refs = refs[:RATE]
        late_refs = refs[RATE : 2 * RATE]
        w_ref, out_ref, comp_ref = refs[2 * RATE :]
        seg = place[0]
        weight = w_ref[...].astype(F32)
        for a in range(RATE):
            comp_ref[a * n : (a + 1) * n, :] = late_refs[a][...]
        pad = n_comp - RATE * n
        row = lax.broadcasted_iota(jnp.int32, (pad, 1), 0)
        extra = jnp.zeros((pad, 2 * width), F32)
        for k, b in enumerate(slots.joints):
            at = slots.late[b]
            tail = late_refs[b][...].astype(F32)
            parts = [tail[at + i : at + i + 1] for i in range(slots.tail[b])]
            at = slots.early[b + 1]
            head = early_refs[b + 1][...].astype(F32)
            parts += [head[at + i : at + i + 1] for i in range(slots.offset[b + 1])]
            slot = sum(p * weight[r : r + 1] for r, p in enumerate(parts))
            extra = jnp.where(row == k, slot, extra)
        comp_ref[RATE * n :, :] = extra.astype(BF16)
        spans = [(a * n, slots.late[a]) for a in range(RATE)] + [(RATE * n, len(slots.joints))]
        comp_bias = slot_bias(seg, n_comp, spans)
        mem_bias = jnp.where(seg >= 1, 0.0, NEG).astype(F32)
        for h in range(heads):
            kc = slice(h * DH, (h + 1) * DH)
            vc = slice(width + h * DH, width + (h + 1) * DH)
            q = q_ref[:, kc]
            pieces = [
                (score(q, comp_ref[:, kc]) + comp_bias, comp_ref, vc),
                (score(q, mem_ref[:, kc]) + mem_bias, mem_ref, vc),
            ]
            so_far = (
                stat_ref[:, 2 * h : 2 * h + 1],
                stat_ref[:, 2 * h + 1 : 2 * h + 2],
                mix_ref[:, kc],
            )
            _, norm, mixed = gathered(pieces, so_far)
            out_ref[:, kc] = (mixed / norm).astype(BF16)

    outs = [((rows, width), BF16)]
    scratch = [pltpu.VMEM((n_comp, 2 * width), BF16)]
    args = [place, q, *begun, memory, *heads_of, *late, weight]
    return call(body, outs, args, scratch)[0]


def output_begin(place, ctx, w_full, xored):
    rows = ctx[0].shape[0]

    def body(place, *refs):
        w_ref, acc_ref = refs[len(ctx) :]
        acc_ref[...] = output_sum(place, refs[: len(ctx)], range(len(ctx)), w_ref, xored)

    outs = [((rows, w_full.shape[1]), F32)]
    return call(body, outs, [place, *ctx, w_full])[0]


def output_sum(place, ctx, steps, w_ref, xored):
    width = ctx[0].shape[1]
    unit = xored or width
    acc = None
    for t, c in zip(steps, ctx):
        for k in range(width // unit):
            block = place[1 + t] * (width // unit) + k
            if xored:
                block = lax.bitwise_xor(block, place[0])
            start = pl.multiple_of(block * unit, unit)
            part = jnp.dot(
                c[:, k * unit : (k + 1) * unit],
                w_ref[pl.ds(start, unit), :],
                preferred_element_type=F32,
            )
            acc = part if acc is None else acc + part
    return acc


def output_end(place, half, n_half, last_step, ctx, begun, w_full, xored, result):
    rows = ctx.shape[0]
    columns = w_full.shape[1]
    n_in = 5 if result is not None else 4

    def body(place, ctx_ref, acc_ref, w_ref, *refs):
        out_ref, held, sem = refs[n_in - 4 :]
        acc = acc_ref[...] + output_sum(place, [ctx_ref], [last_step], w_ref, xored)
        held[...] = acc.astype(BF16)
        copy = pltpu.make_async_copy(held, out_ref.at[pl.ds(half * rows, rows), :], sem)
        copy.start()
        copy.wait()

    args = [place, ctx, begun, w_full]
    in_specs = [smem(), vmem(), vmem(), vmem()]
    aliases = {}
    if result is not None:
        args.append(result)
        in_specs.append(pl.BlockSpec(memory_space=pl.ANY))
        aliases = {4: 0}
    return pl.pallas_call(
        body,
        out_shape=jax.ShapeDtypeStruct((rows * n_half, columns), BF16),
        in_specs=in_specs,
        out_specs=pl.BlockSpec(memory_space=pl.ANY),
        scratch_shapes=[pltpu.VMEM((rows, columns), BF16), pltpu.SemaphoreType.DMA],
        input_output_aliases=aliases,
        compiler_params=params(),
    )(*args)


def gather_rows(block, by_xor):
    size = lax.axis_size("seg")
    if size & (size - 1):
        return lax.all_gather(block, "seg", axis=0, tiled=True)
    seg = lax.axis_index("seg")
    step = 1
    while step < size:
        other = lax.ppermute(block, "seg", [(i, i ^ step) for i in range(size)])
        if by_xor:
            block = jnp.concatenate([block, other], axis=0)
        else:
            upper = (seg // step) % 2 == 1
            low = jnp.where(upper, other, block)
            high = jnp.where(upper, block, other)
            block = jnp.concatenate([low, high], axis=0)
        step *= 2
    return block


def local(layer_input, w_qkv, comp_weight, w_out):
    n_head = lax.axis_size("head")
    seg_len = layer_input.shape[1]
    rows = layer_input[0]
    w3 = jnp.transpose(w_qkv, (1, 0, 2))
    width = w_qkv.shape[2]
    weight = comp_weight.reshape(RATE, 2 * width)
    place = whereabouts()

    n_chunk, n_half = 4, 2
    per_half = n_chunk // n_half
    piece = seg_len // n_chunk
    half_rows = seg_len // n_half
    slots = Slots(seg_len, half_rows)

    def pieces(source, half):
        starts = [(half * per_half + c) * piece for c in range(per_half)]
        return [[lax.slice_in_dim(source, at, at + piece, axis=0)] for at in starts]

    n_seg = lax.axis_size("seg")
    own_rows = w_out.shape[0]
    power = n_seg & (n_seg - 1) == 0
    xored = own_rows if power and own_rows % DH == 0 and width % own_rows == 0 else 0

    w_vmem, col_sums = fetch_weights(w3)
    first = pieces(rows, 0)
    for _ in range(1, n_head):
        for chunk in first:
            chunk.append(around(chunk[-1]))
    w_full = gather_rows(w_out, xored)
    q0, kv0 = project(place, first, w_vmem, col_sums)
    early_parts = compress_early(slots, place, kv0, weight)
    mem0 = passed_along(kv0, 1)
    early = [passed_along(p, BACK - a) for a, p in enumerate(early_parts)]

    second = pieces(after(rows, first[0][1]), 1)
    for _ in range(1, n_head):
        for chunk in second:
            chunk.append(around(chunk[-1]))
    begun = project_begin(place, [chunk[:-1] for chunk in second], w_vmem)
    lasts = [chunk[-1] for chunk in second]
    q1, kv1, *late = project_end(slots, place, lasts, begun, w_vmem, col_sums, kv0, weight)
    mem1 = passed_along(kv1, 1)
    late = [passed_along(p, BACK - a) for a, p in enumerate(late)]

    rings = []
    for q, own in ((q0, [kv0]), (q1, [kv0, kv1])):
        part = attend_begin(slots, place, q, own, mem0, early)
        ctx = attend_end(slots, place, q, part, mem1, early, late, weight)
        rings.append([ctx])
    for _ in range(1, n_head):
        for ring in rings:
            ring.append(around(ring[-1]))
    result = None
    for h, ring in enumerate(rings):
        part = output_begin(place, ring[:-1], w_full, xored)
        result = output_end(place, h, n_half, n_head - 1, ring[-1], part, w_full, xored, result)
    return result[None]


def solution(mesh):
    return jax.shard_map(
        local,
        mesh=mesh,
        in_specs=(
            P(None, "seg", "head"),
            P(None, None, "head"),
            P(None, None, "head"),
            P("seg", "head"),
        ),
        out_specs=P(None, "seg", "head"),
        check_vma=False,
    )
```

```python
import math

import jax
import jax.numpy as jnp
from jax import lax
from jax.experimental import pallas as pl
from jax.experimental.pallas import tpu as pltpu
from jax.sharding import PartitionSpec as P


DH = 128
RATE = 3
BACK = 4
BF16 = jnp.bfloat16
F32 = jnp.float32
NEG = -1e30
VMEM_LIMIT = 14 * 1024 * 1024


def params():
    return pltpu.CompilerParams(vmem_limit_bytes=VMEM_LIMIT)


def vmem():
    return pl.BlockSpec(memory_space=pltpu.VMEM)


def ring_order(size):
    return list(range(size))


def around(block):
    order = ring_order(lax.axis_size("head"))
    route = [(a, b) for a, b in zip(order, order[1:] + order[:1])]
    return lax.ppermute(block, "head", route)


def passed_along(block, distance):
    size = lax.axis_size("seg")
    route = [(i, (i + distance) % size) for i in range(size)]
    return lax.ppermute(block, "seg", route)


def source_of(step, size):
    order = ring_order(size)
    z = lax.axis_index("head")
    found = jnp.int32(0)
    for here in range(size):
        found = jnp.where(z == here, order[(order.index(here) - step) % size], found)
    return found


def hbm():
    return pl.BlockSpec(memory_space=pltpu.HBM)


def call(body, outs, args, scratch=(), in_specs=None):
    return pl.pallas_call(
        body,
        out_shape=tuple(jax.ShapeDtypeStruct(s, d) for s, d in outs),
        in_specs=in_specs or [vmem()] * len(args),
        out_specs=tuple(vmem() for _ in outs),
        scratch_shapes=list(scratch),
        compiler_params=params(),
    )(*args)


def split(rows, starts, piece):
    def body(src, *refs):
        sems = refs[-1]
        copies = [
            pltpu.make_async_copy(src.at[pl.ds(at, piece), :], out, sems.at[i])
            for i, (at, out) in enumerate(zip(starts, refs))
        ]
        for copy in copies:
            copy.start()
        for copy in copies:
            copy.wait()

    outs = [((piece, rows.shape[1]), rows.dtype)] * len(starts)
    scratch = [pltpu.SemaphoreType.DMA((len(starts),))]
    return call(body, outs, [rows], scratch, [hbm()])


def join(one, two):
    n = one.shape[0]

    def body(one_ref, two_ref, out_ref):
        out_ref[:n, :] = one_ref[...]
        out_ref[n:, :] = two_ref[...]

    return call(body, [((2 * n, one.shape[1]), one.dtype)], [one, two])[0]


def weight_rows(w_ref, i, source, feats):
    start = pl.multiple_of(source * feats, feats)
    return w_ref[i, pl.ds(start, feats), :]


def moments(block):
    x = block.astype(F32)
    total = jnp.sum(x, axis=1, keepdims=True)
    off = x - total / x.shape[1]
    return total, jnp.sum(off * off, axis=1, keepdims=True)


def joined_moments(parts, feats):
    count = feats * len(parts)
    mean = sum(t for t, _ in parts) / count
    square = sum(q + feats * jnp.square(t / feats - mean) for t, q in parts)
    return mean, lax.rsqrt(square / count + 1e-05)


def project_sum(blocks, steps, w_ref, i):
    feats = blocks[0].shape[1]
    size = w_ref.shape[1] // feats
    acc = None
    for t, block in zip(steps, blocks):
        part = jnp.dot(
            block[...], weight_rows(w_ref, i, source_of(t, size), feats), preferred_element_type=F32
        )
        acc = part if acc is None else acc + part
    return acc


def fetch_weights(w3):
    n_kind, _, width = w3.shape

    def body(src, w_ref, sum_ref, sems):
        copies = [
            pltpu.make_async_copy(src.at[i], w_ref.at[i], sems.at[i]) for i in range(n_kind)
        ]
        for copy in copies:
            copy.start()
        for i, copy in enumerate(copies):
            copy.wait()
            total = jnp.sum(w_ref[i].astype(F32), axis=0, keepdims=True)
            sum_ref[:, i * width : (i + 1) * width] = jnp.broadcast_to(total, (8, width))

    return pl.pallas_call(
        body,
        out_shape=(
            jax.ShapeDtypeStruct(w3.shape, w3.dtype),
            jax.ShapeDtypeStruct((8, n_kind * width), F32),
        ),
        in_specs=[hbm()],
        out_specs=(vmem(), vmem()),
        scratch_shapes=[pltpu.SemaphoreType.DMA((n_kind,))],
        compiler_params=params(),
        name="fetch",
    )(w3)


def project(chunks, w3, col_sums):
    n_head, n_chunk = len(chunks[0]), len(chunks)
    piece, feats = chunks[0][0].shape
    width = w3.shape[2]
    rows = piece * n_chunk

    def body(*refs):
        w_ref, sum_ref, q_ref, kv_ref = refs[n_head * n_chunk :]
        for c in range(n_chunk):
            blocks = refs[c * n_head : (c + 1) * n_head]
            mean, inv = joined_moments([moments(b[...]) for b in blocks], feats)
            at = pl.ds(c * piece, piece)
            for i in range(3):
                acc = project_sum(blocks, range(n_head), w_ref, i)
                cols = slice(i * width, (i + 1) * width)
                acc = ((acc - mean * sum_ref[0:1, cols]) * inv).astype(BF16)
                if i == 0:
                    q_ref[at, :] = acc
                else:
                    kv_ref[at, (i - 1) * width : i * width] = acc

    flat = [b for chunk in chunks for b in chunk]
    outs = [((rows, width), BF16), ((rows, 2 * width), BF16)]
    return call(body, outs, [*flat, w3, col_sums])


def project_begin(chunks, w3):
    n_here, n_chunk = len(chunks[0]), len(chunks)
    piece, _ = chunks[0][0].shape
    width = w3.shape[2]

    def body(*refs):
        w_ref, acc_ref, mom_ref = refs[n_here * n_chunk :]
        lane = lax.broadcasted_iota(jnp.int32, (piece, 128), 1)
        for c in range(n_chunk):
            blocks = refs[c * n_here : (c + 1) * n_here]
            at = pl.ds(c * piece, piece)
            for i in range(3):
                acc_ref[at, i * width : (i + 1) * width] = project_sum(
                    blocks, range(n_here), w_ref, i
                )
            held = jnp.zeros((piece, 128), F32)
            for t, block in enumerate(blocks):
                for k, value in enumerate(moments(block[...])):
                    held = jnp.where(lane == 2 * t + k, value, held)
            mom_ref[at, :] = held

    flat = [b for chunk in chunks for b in chunk]
    outs = [((piece * n_chunk, 3 * width), F32), ((piece * n_chunk, 128), F32)]
    return call(body, outs, [*flat, w3])


def project_end(slots, lasts, begun, w3, col_sums, before, weight):
    n_chunk = len(lasts)
    piece, feats = lasts[0].shape
    width = w3.shape[2]
    rows = piece * n_chunk
    n_head = w3.shape[1] // feats
    last = n_head - 1

    def body(*refs):
        w_ref, acc_ref, mom_ref, sum_ref, before_ref, cw_ref = refs[n_chunk : n_chunk + 6]
        q_ref, kv_ref, *outs = refs[n_chunk + 6 :]
        for c in range(n_chunk):
            at = pl.ds(c * piece, piece)
            held = mom_ref[at, :]
            parts = [(held[:, 2 * t : 2 * t + 1], held[:, 2 * t + 1 : 2 * t + 2]) for t in range(last)]
            parts.append(moments(refs[c][...]))
            mean, inv = joined_moments(parts, feats)
            for i in range(3):
                cols = slice(i * width, (i + 1) * width)
                acc = acc_ref[at, cols] + project_sum([refs[c]], [last], w_ref, i)
                acc = ((acc - mean * sum_ref[0:1, cols]) * inv).astype(BF16)
                if i == 0:
                    q_ref[at, :] = acc
                else:
                    kv_ref[at, (i - 1) * width : i * width] = acc
        write_slots(slots, True, [before_ref, kv_ref], cw_ref, outs)

    outs = [((rows, width), BF16), ((rows, 2 * width), BF16)]
    outs += [((slots.rows, 2 * width), BF16)] * RATE
    args = [*lasts, w3, *begun, col_sums, before, weight]
    return call(body, outs, args)


class Slots:
    def __init__(self, seg_len, early_rows):
        self.seg_len, self.early_rows = seg_len, early_rows
        self.offset = [(-a * seg_len) % RATE for a in range(RATE)]
        self.count = [(seg_len - o) // RATE for o in self.offset]
        self.tail = [seg_len - o - RATE * n for o, n in zip(self.offset, self.count)]
        self.early = [max(0, (early_rows - o) // RATE) for o in self.offset]
        self.late = [n - e for n, e in zip(self.count, self.early)]
        most = max(
            max(e + o for e, o in zip(self.early, self.offset)),
            max(l + t for l, t in zip(self.late, self.tail)),
        )
        self.rows = -(-most // 16) * 16
        self.joints = [b for b in range(RATE - 1) if self.tail[b] > 0]


def filter_rows(w_ref):
    return [
        jnp.concatenate([w_ref[r, k : k + 1, :].astype(F32) for k in range(2)], axis=1)
        for r in range(RATE)
    ]


def write_slots(slots, late, sources, w_ref, outs):
    weight = filter_rows(w_ref)
    n = slots.rows
    main = sources[-1]
    base = slots.early_rows if late else 0
    counts = slots.late if late else slots.early
    begins = slots.early if late else [0] * RATE
    firsts = [slots.offset[a] + RATE * begins[a] for a in range(RATE)]
    wanted = sorted({f + r for f in firsts for r in range(RATE)})

    def hits(first, rows, at):
        row = lax.broadcasted_iota(jnp.int32, (n, rows), 0)
        col = lax.broadcasted_iota(jnp.int32, (n, rows), 1) + at
        return jnp.where(col == first + RATE * row, 1.0, 0.0).astype(BF16)

    chosen = jnp.concatenate([hits(f, main.shape[0], base) for f in wanted], axis=0)
    picks = jnp.dot(chosen, main[...], preferred_element_type=F32)
    row = lax.broadcasted_iota(jnp.int32, (n, 1), 0)
    picked = {}
    for k, f in enumerate(wanted):
        got = picks[k * n : (k + 1) * n]
        if f < base:
            back = base - f
            got = jnp.where(row == 0, sources[0][-16:, :].astype(F32)[16 - back : 17 - back], got)
        picked[f] = got
    raw = main[...].astype(F32)
    for a in range(RATE):
        acc = None
        for r in range(RATE):
            term = picked[firsts[a] + r] * weight[r]
            acc = term if acc is None else acc + term
        n_raw = slots.tail[a] if late else slots.offset[a]
        for i in range(n_raw):
            at = main.shape[0] - n_raw + i if late else i
            acc = jnp.where(row == counts[a] + i, raw[at : at + 1, :], acc)
        outs[a][...] = acc.astype(BF16)


def compress_early(slots, source, weight):
    def body(source_ref, w_ref, *outs):
        write_slots(slots, False, [source_ref], w_ref, outs)

    outs = [((slots.rows, 2 * weight.shape[2]), BF16)] * RATE
    return call(body, outs, [source, weight])


SCALE = math.log2(math.e) / math.sqrt(DH)


def score(q, keys):
    return lax.dot_general(q, keys, (((1,), (1,)), ((), ())), preferred_element_type=F32)


def slot_bias(seg, n_cols, spans):
    col = lax.broadcasted_iota(jnp.int32, (1, n_cols), 1)
    valid = col < 0
    for begin, count in spans:
        valid |= (col >= begin) & (col < begin + count)
    return jnp.where(valid & (seg >= BACK), 0.0, NEG).astype(F32)


def attend_begin(slots, q, own, memory, early):
    rows, width = q.shape
    n = slots.rows
    n_comp = -(-RATE * n // 128) * 128
    heads = width // DH

    def body(q_ref, *refs):
        own_refs = refs[: len(own)]
        mem_ref = refs[len(own)]
        early_refs = refs[len(own) + 1 : len(own) + 1 + RATE]
        mix_ref, stat_ref, comp_ref = refs[len(own) + 1 + RATE :]
        seg = lax.axis_index("seg")
        for a in range(RATE):
            comp_ref[a * n : (a + 1) * n, :] = early_refs[a][...]
        if n_comp > RATE * n:
            comp_ref[RATE * n :, :] = jnp.zeros((n_comp - RATE * n, 2 * width), BF16)
        comp_bias = slot_bias(seg, n_comp, [(a * n, slots.early[a]) for a in range(RATE)])
        mem_bias = jnp.where(seg >= 1, 0.0, NEG).astype(F32)
        q_row = lax.broadcasted_iota(jnp.int32, (rows, rows), 0)
        k_row = lax.broadcasted_iota(jnp.int32, (rows, rows), 1)
        causal = k_row <= q_row
        lane = lax.broadcasted_iota(jnp.int32, (rows, 128), 1)
        stats = jnp.zeros((rows, 128), F32)
        for h in range(heads):
            kc = slice(h * DH, (h + 1) * DH)
            vc = slice(width + h * DH, width + (h + 1) * DH)
            q = q_ref[:, kc]
            pieces = [
                (score(q, comp_ref[:, kc]) + comp_bias, comp_ref, vc),
                (score(q, mem_ref[:, kc]) + mem_bias, mem_ref, vc),
            ]
            for o in own_refs[:-1]:
                pieces.append((score(q, o[:, kc]), o, vc))
            o = own_refs[-1]
            pieces.append((jnp.where(causal, score(q, o[:, kc]), NEG), o, vc))
            top, norm, mixed = gathered(pieces, None)
            mix_ref[:, kc] = mixed
            stats = jnp.where(lane == 2 * h, top, stats)
            stats = jnp.where(lane == 2 * h + 1, norm, stats)
        stat_ref[...] = stats

    outs = [((rows, width), F32), ((rows, 128), F32)]
    scratch = [pltpu.VMEM((n_comp, 2 * width), BF16)]
    return call(body, outs, [q, *own, memory, *early], scratch)


def gathered(pieces, so_far):
    top = None if so_far is None else so_far[0]
    for s, _, _ in pieces:
        m = jnp.max(s, axis=1, keepdims=True)
        top = m if top is None else jnp.maximum(top, m)
    norm = mixed = None
    if so_far is not None:
        shrink = jnp.exp2((so_far[0] - top) * SCALE)
        norm, mixed = so_far[1] * shrink, so_far[2] * shrink
    for s, v, cols in pieces:
        p = jnp.exp2((s - top) * SCALE)
        total = jnp.sum(p, axis=1, keepdims=True)
        part = jnp.dot(p.astype(BF16), v[:, cols], preferred_element_type=F32)
        norm = total if norm is None else norm + total
        mixed = part if mixed is None else mixed + part
    return top, norm, mixed


def attend_end(slots, q, begun, memory, heads_of, late, weight):
    rows, width = q.shape
    n = slots.rows
    n_comp = -(-(RATE * n + 16) // 128) * 128
    heads = width // DH

    def body(q_ref, mix_ref, stat_ref, mem_ref, *refs):
        early_refs = refs[:RATE]
        late_refs = refs[RATE : 2 * RATE]
        w_ref, out_ref, comp_ref = refs[2 * RATE :]
        seg = lax.axis_index("seg")
        weight = filter_rows(w_ref)
        for a in range(RATE):
            comp_ref[a * n : (a + 1) * n, :] = late_refs[a][...]
        pad = n_comp - RATE * n
        row = lax.broadcasted_iota(jnp.int32, (pad, 1), 0)
        extra = jnp.zeros((pad, 2 * width), F32)
        for k, b in enumerate(slots.joints):
            at = slots.late[b]
            tail = late_refs[b][...].astype(F32)
            parts = [tail[at + i : at + i + 1] for i in range(slots.tail[b])]
            at = slots.early[b + 1]
            head = early_refs[b + 1][...].astype(F32)
            parts += [head[at + i : at + i + 1] for i in range(slots.offset[b + 1])]
            slot = sum(p * weight[r] for r, p in enumerate(parts))
            extra = jnp.where(row == k, slot, extra)
        comp_ref[RATE * n :, :] = extra.astype(BF16)
        spans = [(a * n, slots.late[a]) for a in range(RATE)] + [(RATE * n, len(slots.joints))]
        comp_bias = slot_bias(seg, n_comp, spans)
        mem_bias = jnp.where(seg >= 1, 0.0, NEG).astype(F32)
        for h in range(heads):
            kc = slice(h * DH, (h + 1) * DH)
            vc = slice(width + h * DH, width + (h + 1) * DH)
            q = q_ref[:, kc]
            pieces = [
                (score(q, comp_ref[:, kc]) + comp_bias, comp_ref, vc),
                (score(q, mem_ref[:, kc]) + mem_bias, mem_ref, vc),
            ]
            so_far = (
                stat_ref[:, 2 * h : 2 * h + 1],
                stat_ref[:, 2 * h + 1 : 2 * h + 2],
                mix_ref[:, kc],
            )
            _, norm, mixed = gathered(pieces, so_far)
            out_ref[:, kc] = (mixed / norm).astype(BF16)

    outs = [((rows, width), BF16)]
    scratch = [pltpu.VMEM((n_comp, 2 * width), BF16)]
    args = [q, *begun, memory, *heads_of, *late, weight]
    return call(body, outs, args, scratch)[0]


def output_begin(ctx, w_full, xored):
    rows = ctx[0].shape[0]

    def body(*refs):
        w_ref, acc_ref = refs[len(ctx) :]
        acc_ref[...] = output_sum(refs[: len(ctx)], range(len(ctx)), w_ref, xored)

    outs = [((rows, w_full.shape[1]), F32)]
    return call(body, outs, [*ctx, w_full])[0]


def output_sum(ctx, steps, w_ref, xored):
    width = ctx[0].shape[1]
    unit = xored or width
    size = w_ref.shape[0] // width
    acc = None
    for t, c in zip(steps, ctx):
        for k in range(width // unit):
            block = source_of(t, size) * (width // unit) + k
            if xored:
                block = lax.bitwise_xor(block, lax.axis_index("seg"))
            start = pl.multiple_of(block * unit, unit)
            part = jnp.dot(
                c[:, k * unit : (k + 1) * unit],
                w_ref[pl.ds(start, unit), :],
                preferred_element_type=F32,
            )
            acc = part if acc is None else acc + part
    return acc


def output_end(half, n_half, last_step, ctx, begun, w_full, xored, result):
    rows = ctx.shape[0]
    columns = w_full.shape[1]
    n_extra = 1 if result is not None else 0

    def body(ctx_ref, acc_ref, w_ref, *refs):
        out_ref, held, sem = refs[n_extra:]
        acc = acc_ref[...] + output_sum([ctx_ref], [last_step], w_ref, xored)
        held[...] = acc.astype(BF16)
        copy = pltpu.make_async_copy(held, out_ref.at[pl.ds(half * rows, rows), :], sem)
        copy.start()
        copy.wait()

    args = [ctx, begun, w_full]
    in_specs = [vmem(), vmem(), vmem()]
    aliases = {}
    if result is not None:
        args.append(result)
        in_specs.append(hbm())
        aliases = {3: 0}
    return pl.pallas_call(
        body,
        out_shape=jax.ShapeDtypeStruct((rows * n_half, columns), BF16),
        in_specs=in_specs,
        out_specs=hbm(),
        scratch_shapes=[pltpu.VMEM((rows, columns), BF16), pltpu.SemaphoreType.DMA],
        input_output_aliases=aliases,
        compiler_params=params(),
    )(*args)


def gather_rows(block, by_xor):
    size = lax.axis_size("seg")
    if size & (size - 1):
        return lax.all_gather(block, "seg", axis=0, tiled=True)
    seg = lax.axis_index("seg")
    step = 1
    while step < size:
        other = lax.ppermute(block, "seg", [(i, i ^ step) for i in range(size)])
        if by_xor:
            block = join(block, other)
        else:
            upper = (seg // step) % 2 == 1
            low = jnp.where(upper, other, block)
            high = jnp.where(upper, block, other)
            block = jnp.concatenate([low, high], axis=0)
        step *= 2
    return block


def local(layer_input, w_qkv, comp_weight, w_out):
    n_head = lax.axis_size("head")
    seg_len = layer_input.shape[1]
    rows = pltpu.with_memory_space_constraint(layer_input[0], pltpu.HBM)
    w3 = pltpu.with_memory_space_constraint(jnp.transpose(w_qkv, (1, 0, 2)), pltpu.HBM)
    width = w_qkv.shape[2]
    weight = comp_weight

    n_chunk, n_half = 4, 2
    per_half = n_chunk // n_half
    piece = seg_len // n_chunk
    half_rows = seg_len // n_half
    slots = Slots(seg_len, half_rows)

    starts = [c * piece for c in range(n_chunk)]
    first = [[chunk] for chunk in split(rows, starts[:per_half], piece)]
    n_seg = lax.axis_size("seg")
    own_rows = w_out.shape[0]
    power = n_seg & (n_seg - 1) == 0
    xored = own_rows if power and own_rows % DH == 0 and width % own_rows == 0 else 0

    w_vmem, col_sums = fetch_weights(w3)
    for _ in range(1, n_head):
        for chunk in first:
            chunk.append(around(chunk[-1]))
    w_full = gather_rows(w_out, xored)
    q0, kv0 = project(first, w_vmem, col_sums)
    early_parts = compress_early(slots, kv0, weight)
    mem0 = passed_along(kv0, 1)
    early = [passed_along(p, BACK - a) for a, p in enumerate(early_parts)]

    second = [[chunk] for chunk in split(rows, starts[per_half:], piece)]
    for _ in range(1, n_head):
        for chunk in second:
            chunk.append(around(chunk[-1]))
    begun = project_begin([chunk[:-1] for chunk in second], w_vmem)
    lasts = [chunk[-1] for chunk in second]
    q1, kv1, *late = project_end(slots, lasts, begun, w_vmem, col_sums, kv0, weight)
    mem1 = passed_along(kv1, 1)
    late = [passed_along(p, BACK - a) for a, p in enumerate(late)]

    rings = []
    for q, own in ((q0, [kv0]), (q1, [kv0, kv1])):
        part = attend_begin(slots, q, own, mem0, early)
        ctx = attend_end(slots, q, part, mem1, early, late, weight)
        rings.append([ctx])
    for _ in range(1, n_head):
        for ring in rings:
            ring.append(around(ring[-1]))
    result = None
    for h, ring in enumerate(rings):
        part = output_begin(ring[:-1], w_full, xored)
        result = output_end(h, n_half, n_head - 1, ring[-1], part, w_full, xored, result)
    return result[None]


def solution(mesh):
    return jax.shard_map(
        local,
        mesh=mesh,
        in_specs=(
            P(None, "seg", "head"),
            P(None, None, "head"),
            P(None, None, "head"),
            P("seg", "head"),
        ),
        out_specs=P(None, "seg", "head"),
        check_vma=False,
    )
```

```python
import math

import jax
import jax.numpy as jnp
from jax import lax
from jax.experimental import pallas as pl
from jax.experimental.pallas import tpu as pltpu
from jax.sharding import PartitionSpec as P


DH = 128
RATE = 3
BACK = 4
BF16 = jnp.bfloat16
F32 = jnp.float32
NEG = -1e30
VMEM_LIMIT = 14 * 1024 * 1024


def params():
    return pltpu.CompilerParams(vmem_limit_bytes=VMEM_LIMIT)


def vmem():
    return pl.BlockSpec(memory_space=pltpu.VMEM)


def ring_order(size):
    ups = [i for i in range(size) if i % 2 == 1]
    downs = [i for i in range(size) if i % 2 == 0 and i > 0]
    return [0] + ups + downs[::-1]


def around(block):
    order = ring_order(lax.axis_size("head"))
    route = [(a, b) for a, b in zip(order, order[1:] + order[:1])]
    return lax.ppermute(block, "head", route)


def passed_along(block, distance):
    size = lax.axis_size("seg")
    route = [(i, (i + distance) % size) for i in range(size)]
    return lax.ppermute(block, "seg", route)


def source_of(step, size):
    order = ring_order(size)
    z = lax.axis_index("head")
    found = jnp.int32(0)
    for here in range(size):
        found = jnp.where(z == here, order[(order.index(here) - step) % size], found)
    return found


def hbm():
    return pl.BlockSpec(memory_space=pltpu.HBM)


def call(body, outs, args, scratch=(), in_specs=None):
    return pl.pallas_call(
        body,
        out_shape=tuple(jax.ShapeDtypeStruct(s, d) for s, d in outs),
        in_specs=in_specs or [vmem()] * len(args),
        out_specs=tuple(vmem() for _ in outs),
        scratch_shapes=list(scratch),
        compiler_params=params(),
    )(*args)


def split(rows, starts, piece):
    def body(src, *refs):
        sems = refs[-1]
        copies = [
            pltpu.make_async_copy(src.at[pl.ds(at, piece), :], out, sems.at[i])
            for i, (at, out) in enumerate(zip(starts, refs))
        ]
        for copy in copies:
            copy.start()
        for copy in copies:
            copy.wait()

    outs = [((piece, rows.shape[1]), rows.dtype)] * len(starts)
    scratch = [pltpu.SemaphoreType.DMA((len(starts),))]
    return call(body, outs, [rows], scratch, [hbm()])


def join(one, two):
    n = one.shape[0]

    def body(one_ref, two_ref, out_ref):
        out_ref[:n, :] = one_ref[...]
        out_ref[n:, :] = two_ref[...]

    return call(body, [((2 * n, one.shape[1]), one.dtype)], [one, two])[0]


def weight_rows(w_ref, i, source, feats):
    start = pl.multiple_of(source * feats, feats)
    return w_ref[i, pl.ds(start, feats), :]


def moments(block):
    x = block.astype(F32)
    total = jnp.sum(x, axis=1, keepdims=True)
    off = x - total / x.shape[1]
    return total, jnp.sum(off * off, axis=1, keepdims=True)


def joined_moments(parts, feats):
    count = feats * len(parts)
    mean = sum(t for t, _ in parts) / count
    square = sum(q + feats * jnp.square(t / feats - mean) for t, q in parts)
    return mean, lax.rsqrt(square / count + 1e-05)


def project_sum(blocks, steps, w_ref, i):
    feats = blocks[0].shape[1]
    size = w_ref.shape[1] // feats
    acc = None
    for t, block in zip(steps, blocks):
        part = jnp.dot(
            block[...], weight_rows(w_ref, i, source_of(t, size), feats), preferred_element_type=F32
        )
        acc = part if acc is None else acc + part
    return acc


def fetch_weights(w3):
    n_kind, _, width = w3.shape

    def body(src, w_ref, sum_ref, sems):
        copies = [
            pltpu.make_async_copy(src.at[i], w_ref.at[i], sems.at[i]) for i in range(n_kind)
        ]
        for copy in copies:
            copy.start()
        for i, copy in enumerate(copies):
            copy.wait()
            total = jnp.sum(w_ref[i].astype(F32), axis=0, keepdims=True)
            sum_ref[:, i * width : (i + 1) * width] = jnp.broadcast_to(total, (8, width))

    return pl.pallas_call(
        body,
        out_shape=(
            jax.ShapeDtypeStruct(w3.shape, w3.dtype),
            jax.ShapeDtypeStruct((8, n_kind * width), F32),
        ),
        in_specs=[hbm()],
        out_specs=(vmem(), vmem()),
        scratch_shapes=[pltpu.SemaphoreType.DMA((n_kind,))],
        compiler_params=params(),
        name="fetch",
    )(w3)


def project(chunks, w3, col_sums):
    n_head, n_chunk = len(chunks[0]), len(chunks)
    piece, feats = chunks[0][0].shape
    width = w3.shape[2]
    rows = piece * n_chunk

    def body(*refs):
        w_ref, sum_ref, q_ref, kv_ref = refs[n_head * n_chunk :]
        for c in range(n_chunk):
            blocks = refs[c * n_head : (c + 1) * n_head]
            mean, inv = joined_moments([moments(b[...]) for b in blocks], feats)
            at = pl.ds(c * piece, piece)
            for i in range(3):
                acc = project_sum(blocks, range(n_head), w_ref, i)
                cols = slice(i * width, (i + 1) * width)
                acc = ((acc - mean * sum_ref[0:1, cols]) * inv).astype(BF16)
                if i == 0:
                    q_ref[at, :] = acc
                else:
                    kv_ref[at, (i - 1) * width : i * width] = acc

    flat = [b for chunk in chunks for b in chunk]
    outs = [((rows, width), BF16), ((rows, 2 * width), BF16)]
    return call(body, outs, [*flat, w3, col_sums])


def project_begin(chunks, w3):
    n_here, n_chunk = len(chunks[0]), len(chunks)
    piece, _ = chunks[0][0].shape
    width = w3.shape[2]

    def body(*refs):
        w_ref, acc_ref, mom_ref = refs[n_here * n_chunk :]
        lane = lax.broadcasted_iota(jnp.int32, (piece, 128), 1)
        for c in range(n_chunk):
            blocks = refs[c * n_here : (c + 1) * n_here]
            at = pl.ds(c * piece, piece)
            for i in range(3):
                acc_ref[at, i * width : (i + 1) * width] = project_sum(
                    blocks, range(n_here), w_ref, i
                )
            held = jnp.zeros((piece, 128), F32)
            for t, block in enumerate(blocks):
                for k, value in enumerate(moments(block[...])):
                    held = jnp.where(lane == 2 * t + k, value, held)
            mom_ref[at, :] = held

    flat = [b for chunk in chunks for b in chunk]
    outs = [((piece * n_chunk, 3 * width), F32), ((piece * n_chunk, 128), F32)]
    return call(body, outs, [*flat, w3])


def project_end(lasts, begun, w3, col_sums, kinds):
    n_chunk = len(lasts)
    piece, feats = lasts[0].shape
    width = w3.shape[2]
    rows = piece * n_chunk
    last = w3.shape[1] // feats - 1

    def body(*refs):
        w_ref, acc_ref, mom_ref, sum_ref, out_ref = refs[n_chunk:]
        for c in range(n_chunk):
            at = pl.ds(c * piece, piece)
            held = mom_ref[at, :]
            parts = [(held[:, 2 * t : 2 * t + 1], held[:, 2 * t + 1 : 2 * t + 2]) for t in range(last)]
            parts.append(moments(refs[c][...]))
            mean, inv = joined_moments(parts, feats)
            for k, i in enumerate(kinds):
                cols = slice(i * width, (i + 1) * width)
                acc = acc_ref[at, cols] + project_sum([refs[c]], [last], w_ref, i)
                acc = (acc - mean * sum_ref[0:1, cols]) * inv
                out_ref[at, k * width : (k + 1) * width] = acc.astype(BF16)

    outs = [((rows, len(kinds) * width), BF16)]
    return call(body, outs, [*lasts, w3, *begun, col_sums])[0]


class Slots:
    def __init__(self, seg_len, early_rows):
        self.seg_len, self.early_rows = seg_len, early_rows
        self.offset = [(-a * seg_len) % RATE for a in range(RATE)]
        self.count = [(seg_len - o) // RATE for o in self.offset]
        self.tail = [seg_len - o - RATE * n for o, n in zip(self.offset, self.count)]
        self.early = [max(0, (early_rows - o) // RATE) for o in self.offset]
        self.late = [n - e for n, e in zip(self.count, self.early)]
        most = max(
            max(e + o for e, o in zip(self.early, self.offset)),
            max(l + t for l, t in zip(self.late, self.tail)),
        )
        self.rows = -(-most // 16) * 16
        self.joints = [b for b in range(RATE - 1) if self.tail[b] > 0]


def filter_rows(w_ref):
    return [
        jnp.concatenate([w_ref[r, k : k + 1, :].astype(F32) for k in range(2)], axis=1)
        for r in range(RATE)
    ]


def write_slots(slots, late, sources, w_ref, outs):
    weight = filter_rows(w_ref)
    n = slots.rows
    main = sources[-1]
    base = slots.early_rows if late else 0
    counts = slots.late if late else slots.early
    begins = slots.early if late else [0] * RATE
    firsts = [slots.offset[a] + RATE * begins[a] for a in range(RATE)]
    wanted = sorted({f + r for f in firsts for r in range(RATE)})

    def hits(first, rows, at):
        row = lax.broadcasted_iota(jnp.int32, (n, rows), 0)
        col = lax.broadcasted_iota(jnp.int32, (n, rows), 1) + at
        return jnp.where(col == first + RATE * row, 1.0, 0.0).astype(BF16)

    chosen = jnp.concatenate([hits(f, main.shape[0], base) for f in wanted], axis=0)
    picks = jnp.dot(chosen, main[...], preferred_element_type=F32)
    row = lax.broadcasted_iota(jnp.int32, (n, 1), 0)
    picked = {}
    for k, f in enumerate(wanted):
        got = picks[k * n : (k + 1) * n]
        if f < base:
            back = base - f
            got = jnp.where(row == 0, sources[0][-16:, :].astype(F32)[16 - back : 17 - back], got)
        picked[f] = got
    raw = main[...].astype(F32)
    for a in range(RATE):
        acc = None
        for r in range(RATE):
            term = picked[firsts[a] + r] * weight[r]
            acc = term if acc is None else acc + term
        n_raw = slots.tail[a] if late else slots.offset[a]
        for i in range(n_raw):
            at = main.shape[0] - n_raw + i if late else i
            acc = jnp.where(row == counts[a] + i, raw[at : at + 1, :], acc)
        outs[a][...] = acc.astype(BF16)


def compress(slots, sources, weight):
    n_in = len(sources)

    def body(*refs):
        write_slots(slots, n_in == 2, refs[:n_in], refs[n_in], refs[n_in + 1 :])

    outs = [((slots.rows, 2 * weight.shape[2]), BF16)] * RATE
    return call(body, outs, [*sources, weight])


SCALE = math.log2(math.e) / math.sqrt(DH)


def score(q, keys):
    return lax.dot_general(q, keys, (((1,), (1,)), ((), ())), preferred_element_type=F32)


def slot_bias(seg, n_cols, spans):
    col = lax.broadcasted_iota(jnp.int32, (1, n_cols), 1)
    valid = col < 0
    for begin, count in spans:
        valid |= (col >= begin) & (col < begin + count)
    return jnp.where(valid & (seg >= BACK), 0.0, NEG).astype(F32)


def attend_begin(slots, q, own, memory, early):
    rows, width = q.shape
    n = slots.rows
    n_comp = -(-RATE * n // 128) * 128
    heads = width // DH

    def body(q_ref, *refs):
        own_refs = refs[: len(own)]
        mem_ref = refs[len(own)]
        early_refs = refs[len(own) + 1 : len(own) + 1 + RATE]
        mix_ref, stat_ref, comp_ref = refs[len(own) + 1 + RATE :]
        seg = lax.axis_index("seg")
        for a in range(RATE):
            comp_ref[a * n : (a + 1) * n, :] = early_refs[a][...]
        if n_comp > RATE * n:
            comp_ref[RATE * n :, :] = jnp.zeros((n_comp - RATE * n, 2 * width), BF16)
        comp_bias = slot_bias(seg, n_comp, [(a * n, slots.early[a]) for a in range(RATE)])
        mem_bias = jnp.where(seg >= 1, 0.0, NEG).astype(F32)
        q_row = lax.broadcasted_iota(jnp.int32, (rows, rows), 0)
        k_row = lax.broadcasted_iota(jnp.int32, (rows, rows), 1)
        causal = k_row <= q_row
        lane = lax.broadcasted_iota(jnp.int32, (rows, 128), 1)
        stats = jnp.zeros((rows, 128), F32)
        for h in range(heads):
            kc = slice(h * DH, (h + 1) * DH)
            vc = slice(width + h * DH, width + (h + 1) * DH)
            q = q_ref[:, kc]
            pieces = [
                (score(q, comp_ref[:, kc]) + comp_bias, comp_ref, vc),
                (score(q, mem_ref[:, kc]) + mem_bias, mem_ref, vc),
            ]
            for o in own_refs[:-1]:
                pieces.append((score(q, o[:, kc]), o, vc))
            o = own_refs[-1]
            pieces.append((jnp.where(causal, score(q, o[:, kc]), NEG), o, vc))
            top, norm, mixed = gathered(pieces, None)
            mix_ref[:, kc] = mixed
            stats = jnp.where(lane == 2 * h, top, stats)
            stats = jnp.where(lane == 2 * h + 1, norm, stats)
        stat_ref[...] = stats

    outs = [((rows, width), F32), ((rows, 128), F32)]
    scratch = [pltpu.VMEM((n_comp, 2 * width), BF16)]
    return call(body, outs, [q, *own, memory, *early], scratch)


def gathered(pieces, so_far):
    top = None if so_far is None else so_far[0]
    for s, _, _ in pieces:
        m = jnp.max(s, axis=1, keepdims=True)
        top = m if top is None else jnp.maximum(top, m)
    norm = mixed = None
    if so_far is not None:
        shrink = jnp.exp2((so_far[0] - top) * SCALE)
        norm, mixed = so_far[1] * shrink, so_far[2] * shrink
    for s, v, cols in pieces:
        p = jnp.exp2((s - top) * SCALE)
        total = jnp.sum(p, axis=1, keepdims=True)
        part = jnp.dot(p.astype(BF16), v[:, cols], preferred_element_type=F32)
        norm = total if norm is None else norm + total
        mixed = part if mixed is None else mixed + part
    return top, norm, mixed


def attend_end(slots, q, begun, memory, heads_of, late, weight):
    rows, width = q.shape
    n = slots.rows
    n_comp = -(-(RATE * n + 16) // 128) * 128
    heads = width // DH

    def body(q_ref, mix_ref, stat_ref, mem_ref, *refs):
        early_refs = refs[:RATE]
        late_refs = refs[RATE : 2 * RATE]
        w_ref, out_ref, comp_ref = refs[2 * RATE :]
        seg = lax.axis_index("seg")
        weight = filter_rows(w_ref)
        for a in range(RATE):
            comp_ref[a * n : (a + 1) * n, :] = late_refs[a][...]
        pad = n_comp - RATE * n
        row = lax.broadcasted_iota(jnp.int32, (pad, 1), 0)
        extra = jnp.zeros((pad, 2 * width), F32)
        for k, b in enumerate(slots.joints):
            at = slots.late[b]
            tail = late_refs[b][...].astype(F32)
            parts = [tail[at + i : at + i + 1] for i in range(slots.tail[b])]
            at = slots.early[b + 1]
            head = early_refs[b + 1][...].astype(F32)
            parts += [head[at + i : at + i + 1] for i in range(slots.offset[b + 1])]
            slot = sum(p * weight[r] for r, p in enumerate(parts))
            extra = jnp.where(row == k, slot, extra)
        comp_ref[RATE * n :, :] = extra.astype(BF16)
        spans = [(a * n, slots.late[a]) for a in range(RATE)] + [(RATE * n, len(slots.joints))]
        comp_bias = slot_bias(seg, n_comp, spans)
        mem_bias = jnp.where(seg >= 1, 0.0, NEG).astype(F32)
        for h in range(heads):
            kc = slice(h * DH, (h + 1) * DH)
            vc = slice(width + h * DH, width + (h + 1) * DH)
            q = q_ref[:, kc]
            pieces = [
                (score(q, comp_ref[:, kc]) + comp_bias, comp_ref, vc),
                (score(q, mem_ref[:, kc]) + mem_bias, mem_ref, vc),
            ]
            so_far = (
                stat_ref[:, 2 * h : 2 * h + 1],
                stat_ref[:, 2 * h + 1 : 2 * h + 2],
                mix_ref[:, kc],
            )
            _, norm, mixed = gathered(pieces, so_far)
            out_ref[:, kc] = (mixed / norm).astype(BF16)

    outs = [((rows, width), BF16)]
    scratch = [pltpu.VMEM((n_comp, 2 * width), BF16)]
    args = [q, *begun, memory, *heads_of, *late, weight]
    return call(body, outs, args, scratch)[0]


def output_begin(ctx, w_full, xored):
    rows = ctx[0].shape[0]

    def body(*refs):
        w_ref, acc_ref = refs[len(ctx) :]
        acc_ref[...] = output_sum(refs[: len(ctx)], range(len(ctx)), w_ref, xored)

    outs = [((rows, w_full.shape[1]), F32)]
    return call(body, outs, [*ctx, w_full])[0]


def output_sum(ctx, steps, w_ref, xored):
    width = ctx[0].shape[1]
    unit = xored or width
    size = w_ref.shape[0] // width
    acc = None
    for t, c in zip(steps, ctx):
        for k in range(width // unit):
            block = source_of(t, size) * (width // unit) + k
            if xored:
                block = lax.bitwise_xor(block, lax.axis_index("seg"))
            start = pl.multiple_of(block * unit, unit)
            part = jnp.dot(
                c[:, k * unit : (k + 1) * unit],
                w_ref[pl.ds(start, unit), :],
                preferred_element_type=F32,
            )
            acc = part if acc is None else acc + part
    return acc


def output_end(half, n_half, last_step, ctx, begun, w_full, xored, result):
    rows = ctx.shape[0]
    columns = w_full.shape[1]
    n_extra = 1 if result is not None else 0
    n_copy = 4 if rows % 64 == 0 else 1
    part = rows // n_copy

    def body(ctx_ref, acc_ref, w_ref, *refs):
        out_ref, held, sems = refs[n_extra:]
        acc = output_sum([ctx_ref], [last_step], w_ref, xored)
        copies = []
        for k in range(n_copy):
            at = pl.ds(k * part, part)
            held[at, :] = (acc_ref[at, :] + acc[k * part : (k + 1) * part]).astype(BF16)
            to = out_ref.at[pl.ds(half * rows + k * part, part), :]
            copies.append(pltpu.make_async_copy(held.at[at, :], to, sems.at[k]))
            copies[-1].start()
        for copy in copies:
            copy.wait()

    args = [ctx, begun, w_full]
    in_specs = [vmem(), vmem(), vmem()]
    aliases = {}
    if result is not None:
        args.append(result)
        in_specs.append(hbm())
        aliases = {3: 0}
    return pl.pallas_call(
        body,
        out_shape=jax.ShapeDtypeStruct((rows * n_half, columns), BF16),
        in_specs=in_specs,
        out_specs=hbm(),
        scratch_shapes=[pltpu.VMEM((rows, columns), BF16), pltpu.SemaphoreType.DMA((n_copy,))],
        input_output_aliases=aliases,
        compiler_params=params(),
    )(*args)


def gather_rows(block, by_xor):
    size = lax.axis_size("seg")
    if size & (size - 1):
        return lax.all_gather(block, "seg", axis=0, tiled=True)
    seg = lax.axis_index("seg")
    step = 1
    while step < size:
        other = lax.ppermute(block, "seg", [(i, i ^ step) for i in range(size)])
        if by_xor:
            block = join(block, other)
        else:
            upper = (seg // step) % 2 == 1
            low = jnp.where(upper, other, block)
            high = jnp.where(upper, block, other)
            block = jnp.concatenate([low, high], axis=0)
        step *= 2
    return block


def local(layer_input, w_qkv, comp_weight, w_out):
    n_head = lax.axis_size("head")
    seg_len = layer_input.shape[1]
    rows = pltpu.with_memory_space_constraint(layer_input[0], pltpu.HBM)
    w3 = pltpu.with_memory_space_constraint(jnp.transpose(w_qkv, (1, 0, 2)), pltpu.HBM)
    width = w_qkv.shape[2]
    weight = comp_weight

    n_chunk, n_half = 4, 2
    per_half = n_chunk // n_half
    piece = seg_len // n_chunk
    half_rows = seg_len // n_half
    slots = Slots(seg_len, half_rows)

    starts = [c * piece for c in range(n_chunk)]
    first = [[chunk] for chunk in split(rows, starts[:per_half], piece)]
    n_seg = lax.axis_size("seg")
    own_rows = w_out.shape[0]
    power = n_seg & (n_seg - 1) == 0
    xored = own_rows if power and own_rows % DH == 0 and width % own_rows == 0 else 0

    w_vmem, col_sums = fetch_weights(w3)
    for _ in range(1, n_head):
        for chunk in first:
            chunk.append(around(chunk[-1]))
    w_full = gather_rows(w_out, xored)
    q0, kv0 = project(first, w_vmem, col_sums)
    early_parts = compress(slots, [kv0], weight)
    mem0 = passed_along(kv0, 1)
    early = [passed_along(p, BACK - a) for a, p in enumerate(early_parts)]

    second = [[chunk] for chunk in split(rows, starts[per_half:], piece)]
    for _ in range(1, n_head):
        for chunk in second:
            chunk.append(around(chunk[-1]))
    begun = project_begin([chunk[:-1] for chunk in second], w_vmem)
    lasts = [chunk[-1] for chunk in second]
    kv1 = project_end(lasts, begun, w_vmem, col_sums, (1, 2))
    mem1 = passed_along(kv1, 1)
    late_parts = compress(slots, [kv0, kv1], weight)
    late = [passed_along(p, BACK - a) for a, p in enumerate(late_parts)]
    q1 = project_end(lasts, begun, w_vmem, col_sums, (0,))

    rings = []
    for q, own in ((q0, [kv0]), (q1, [kv0, kv1])):
        part = attend_begin(slots, q, own, mem0, early)
        ctx = attend_end(slots, q, part, mem1, early, late, weight)
        rings.append([ctx])
    for _ in range(1, n_head):
        for ring in rings:
            ring.append(around(ring[-1]))
    result = None
    for h, ring in enumerate(rings):
        part = output_begin(ring[:-1], w_full, xored)
        result = output_end(h, n_half, n_head - 1, ring[-1], part, w_full, xored, result)
    return result[None]


def solution(mesh):
    return jax.shard_map(
        local,
        mesh=mesh,
        in_specs=(
            P(None, "seg", "head"),
            P(None, None, "head"),
            P(None, None, "head"),
            P("seg", "head"),
        ),
        out_specs=P(None, "seg", "head"),
        check_vma=False,
    )
```

```python
import math

import jax
import jax.numpy as jnp
from jax import lax
from jax.experimental import pallas as pl
from jax.experimental.pallas import tpu as pltpu
from jax.sharding import PartitionSpec as P


DH = 128
RATE = 3
BACK = 4
BF16 = jnp.bfloat16
F32 = jnp.float32
NEG = -1e30
VMEM_LIMIT = 14 * 1024 * 1024


def params():
    return pltpu.CompilerParams(vmem_limit_bytes=VMEM_LIMIT)


def vmem():
    return pl.BlockSpec(memory_space=pltpu.VMEM)


def folded_ring(size):
    ups = [i for i in range(size) if i % 2 == 1]
    downs = [i for i in range(size) if i % 2 == 0 and i > 0]
    return [0] + ups + downs[::-1]


IN_RING = folded_ring
OUT_RING = folded_ring
EARLY = 8
EARLY_PARTS, LATE_PARTS = 2, 2


def around(block, order):
    route = [(a, b) for a, b in zip(order, order[1:] + order[:1])]
    return lax.ppermute(block, "head", route)


def passed_along(block, distance):
    size = lax.axis_size("seg")
    route = [(i, (i + distance) % size) for i in range(size)]
    return lax.ppermute(block, "seg", route)


def source_of(step, order):
    size = len(order)
    z = lax.axis_index("head")
    found = jnp.int32(0)
    for here in range(size):
        found = jnp.where(z == here, order[(order.index(here) - step) % size], found)
    return found


def hbm():
    return pl.BlockSpec(memory_space=pltpu.HBM)


def call(body, outs, args, scratch=(), in_specs=None):
    return pl.pallas_call(
        body,
        out_shape=tuple(jax.ShapeDtypeStruct(s, d) for s, d in outs),
        in_specs=in_specs or [vmem()] * len(args),
        out_specs=tuple(vmem() for _ in outs),
        scratch_shapes=list(scratch),
        compiler_params=params(),
    )(*args)


def split(rows, starts, piece):
    def body(src, *refs):
        sems = refs[-1]
        copies = [
            pltpu.make_async_copy(src.at[pl.ds(at, piece), :], out, sems.at[i])
            for i, (at, out) in enumerate(zip(starts, refs))
        ]
        for copy in copies:
            copy.start()
        for copy in copies:
            copy.wait()

    outs = [((piece, rows.shape[1]), rows.dtype)] * len(starts)
    scratch = [pltpu.SemaphoreType.DMA((len(starts),))]
    return call(body, outs, [rows], scratch, [hbm()])


def join(one, two):
    n = one.shape[0]

    def body(one_ref, two_ref, out_ref):
        out_ref[:n, :] = one_ref[...]
        out_ref[n:, :] = two_ref[...]

    return call(body, [((2 * n, one.shape[1]), one.dtype)], [one, two])[0]


def weight_rows(w_ref, i, source, feats):
    start = pl.multiple_of(source * feats, feats)
    return w_ref[i, pl.ds(start, feats), :]


def moments(block):
    x = block.astype(F32)
    total = jnp.sum(x, axis=1, keepdims=True)
    off = x - total / x.shape[1]
    return total, jnp.sum(off * off, axis=1, keepdims=True)


def joined_moments(parts, feats):
    count = feats * len(parts)
    mean = sum(t for t, _ in parts) / count
    square = sum(q + feats * jnp.square(t / feats - mean) for t, q in parts)
    return mean, lax.rsqrt(square / count + 1e-05)


def project_sum(blocks, steps, w_ref, i):
    feats = blocks[0].shape[1]
    size = w_ref.shape[1] // feats
    acc = None
    for t, block in zip(steps, blocks):
        part = jnp.dot(
            block[...], weight_rows(w_ref, i, source_of(t, IN_RING(size)), feats), preferred_element_type=F32
        )
        acc = part if acc is None else acc + part
    return acc


def fetch_weights(w3):
    n_kind, _, width = w3.shape

    def body(src, w_ref, sum_ref, sems):
        copies = [
            pltpu.make_async_copy(src.at[i], w_ref.at[i], sems.at[i]) for i in range(n_kind)
        ]
        for copy in copies:
            copy.start()
        for i, copy in enumerate(copies):
            copy.wait()
            total = jnp.sum(w_ref[i].astype(F32), axis=0, keepdims=True)
            sum_ref[:, i * width : (i + 1) * width] = jnp.broadcast_to(total, (8, width))

    return pl.pallas_call(
        body,
        out_shape=(
            jax.ShapeDtypeStruct(w3.shape, w3.dtype),
            jax.ShapeDtypeStruct((8, n_kind * width), F32),
        ),
        in_specs=[hbm()],
        out_specs=(vmem(), vmem()),
        scratch_shapes=[pltpu.SemaphoreType.DMA((n_kind,))],
        compiler_params=params(),
        name="fetch",
    )(w3)


def project(chunks, w3, col_sums):
    n_head, n_chunk = len(chunks[0]), len(chunks)
    piece, feats = chunks[0][0].shape
    width = w3.shape[2]
    rows = piece * n_chunk

    def body(*refs):
        w_ref, sum_ref, q_ref, kv_ref = refs[n_head * n_chunk :]
        for c in range(n_chunk):
            blocks = refs[c * n_head : (c + 1) * n_head]
            mean, inv = joined_moments([moments(b[...]) for b in blocks], feats)
            at = pl.ds(c * piece, piece)
            for i in range(3):
                acc = project_sum(blocks, range(n_head), w_ref, i)
                cols = slice(i * width, (i + 1) * width)
                acc = ((acc - mean * sum_ref[0:1, cols]) * inv).astype(BF16)
                if i == 0:
                    q_ref[at, :] = acc
                else:
                    kv_ref[at, (i - 1) * width : i * width] = acc

    flat = [b for chunk in chunks for b in chunk]
    outs = [((rows, width), BF16), ((rows, 2 * width), BF16)]
    return call(body, outs, [*flat, w3, col_sums])


def project_begin(chunks, w3):
    n_here, n_chunk = len(chunks[0]), len(chunks)
    piece, _ = chunks[0][0].shape
    width = w3.shape[2]

    def body(*refs):
        w_ref, acc_ref, mom_ref = refs[n_here * n_chunk :]
        lane = lax.broadcasted_iota(jnp.int32, (piece, 128), 1)
        for c in range(n_chunk):
            blocks = refs[c * n_here : (c + 1) * n_here]
            at = pl.ds(c * piece, piece)
            for i in range(3):
                acc_ref[at, i * width : (i + 1) * width] = project_sum(
                    blocks, range(n_here), w_ref, i
                )
            held = jnp.zeros((piece, 128), F32)
            for t, block in enumerate(blocks):
                for k, value in enumerate(moments(block[...])):
                    held = jnp.where(lane == 2 * t + k, value, held)
            mom_ref[at, :] = held

    flat = [b for chunk in chunks for b in chunk]
    outs = [((piece * n_chunk, 3 * width), F32), ((piece * n_chunk, 128), F32)]
    return call(body, outs, [*flat, w3])


def project_end(lasts, begun, w3, col_sums, kinds):
    n_chunk = len(lasts)
    piece, feats = lasts[0].shape
    width = w3.shape[2]
    rows = piece * n_chunk
    last = w3.shape[1] // feats - 1

    def body(*refs):
        w_ref, acc_ref, mom_ref, sum_ref, out_ref = refs[n_chunk:]
        for c in range(n_chunk):
            at = pl.ds(c * piece, piece)
            held = mom_ref[at, :]
            parts = [(held[:, 2 * t : 2 * t + 1], held[:, 2 * t + 1 : 2 * t + 2]) for t in range(last)]
            parts.append(moments(refs[c][...]))
            mean, inv = joined_moments(parts, feats)
            for k, i in enumerate(kinds):
                cols = slice(i * width, (i + 1) * width)
                acc = acc_ref[at, cols] + project_sum([refs[c]], [last], w_ref, i)
                acc = (acc - mean * sum_ref[0:1, cols]) * inv
                out_ref[at, k * width : (k + 1) * width] = acc.astype(BF16)

    outs = [((rows, len(kinds) * width), BF16)]
    return call(body, outs, [*lasts, w3, *begun, col_sums])[0]


class Slots:
    def __init__(self, seg_len, early_rows):
        self.seg_len, self.early_rows = seg_len, early_rows
        self.offset = [(-a * seg_len) % RATE for a in range(RATE)]
        self.count = [(seg_len - o) // RATE for o in self.offset]
        self.tail = [seg_len - o - RATE * n for o, n in zip(self.offset, self.count)]
        self.early = [max(0, (early_rows - o) // RATE) for o in self.offset]
        self.late = [n - e for n, e in zip(self.count, self.early)]
        most = max(
            max(e + o for e, o in zip(self.early, self.offset)),
            max(l + t for l, t in zip(self.late, self.tail)),
        )
        self.rows = -(-most // 16) * 16
        self.joints = [b for b in range(RATE - 1) if self.tail[b] > 0]


def filter_rows(w_ref):
    return [
        jnp.concatenate([w_ref[r, k : k + 1, :].astype(F32) for k in range(2)], axis=1)
        for r in range(RATE)
    ]


def write_slots(slots, late, sources, w_ref, outs):
    weight = filter_rows(w_ref)
    n = slots.rows
    main = sources[-1]
    base = slots.early_rows if late else 0
    counts = slots.late if late else slots.early
    begins = slots.early if late else [0] * RATE
    firsts = [slots.offset[a] + RATE * begins[a] for a in range(RATE)]
    wanted = sorted({f + r for f in firsts for r in range(RATE)})

    def hits(first, rows, at):
        row = lax.broadcasted_iota(jnp.int32, (n, rows), 0)
        col = lax.broadcasted_iota(jnp.int32, (n, rows), 1) + at
        return jnp.where(col == first + RATE * row, 1.0, 0.0).astype(BF16)

    chosen = jnp.concatenate([hits(f, main.shape[0], base) for f in wanted], axis=0)
    picks = jnp.dot(chosen, main[...], preferred_element_type=F32)
    row = lax.broadcasted_iota(jnp.int32, (n, 1), 0)
    picked = {}
    for k, f in enumerate(wanted):
        got = picks[k * n : (k + 1) * n]
        if f < base:
            back = base - f
            got = jnp.where(row == 0, sources[0][-16:, :].astype(F32)[16 - back : 17 - back], got)
        picked[f] = got
    raw = main[...].astype(F32)
    for a in range(RATE):
        acc = None
        for r in range(RATE):
            term = picked[firsts[a] + r] * weight[r]
            acc = term if acc is None else acc + term
        n_raw = slots.tail[a] if late else slots.offset[a]
        for i in range(n_raw):
            at = main.shape[0] - n_raw + i if late else i
            acc = jnp.where(row == counts[a] + i, raw[at : at + 1, :], acc)
        outs[a][...] = acc.astype(BF16)


def compress(slots, sources, weight):
    n_in = len(sources)

    def body(*refs):
        write_slots(slots, n_in == 2, refs[:n_in], refs[n_in], refs[n_in + 1 :])

    outs = [((slots.rows, 2 * weight.shape[2]), BF16)] * RATE
    return call(body, outs, [*sources, weight])


SCALE = math.log2(math.e) / math.sqrt(DH)


def score(q, keys):
    return lax.dot_general(q, keys, (((1,), (1,)), ((), ())), preferred_element_type=F32)


def slot_bias(seg, n_cols, spans):
    col = lax.broadcasted_iota(jnp.int32, (1, n_cols), 1)
    valid = col < 0
    for begin, count in spans:
        valid |= (col >= begin) & (col < begin + count)
    return jnp.where(valid & (seg >= BACK), 0.0, NEG).astype(F32)


def attend_begin(slots, q, own, memory, early):
    rows, width = q.shape
    n = slots.rows
    n_comp = -(-RATE * n // 128) * 128
    heads = width // DH

    def body(q_ref, *refs):
        own_refs = refs[: len(own)]
        mem_ref = refs[len(own)]
        early_refs = refs[len(own) + 1 : len(own) + 1 + RATE]
        mix_ref, stat_ref, comp_ref = refs[len(own) + 1 + RATE :]
        seg = lax.axis_index("seg")
        for a in range(RATE):
            comp_ref[a * n : (a + 1) * n, :] = early_refs[a][...]
        if n_comp > RATE * n:
            comp_ref[RATE * n :, :] = jnp.zeros((n_comp - RATE * n, 2 * width), BF16)
        comp_bias = slot_bias(seg, n_comp, [(a * n, slots.early[a]) for a in range(RATE)])
        mem_bias = jnp.where(seg >= 1, 0.0, NEG).astype(F32)
        q_row = lax.broadcasted_iota(jnp.int32, (rows, rows), 0)
        k_row = lax.broadcasted_iota(jnp.int32, (rows, rows), 1)
        causal = k_row <= q_row
        lane = lax.broadcasted_iota(jnp.int32, (rows, 128), 1)
        stats = jnp.zeros((rows, 128), F32)
        for h in range(heads):
            kc = slice(h * DH, (h + 1) * DH)
            vc = slice(width + h * DH, width + (h + 1) * DH)
            q = q_ref[:, kc]
            pieces = [
                (score(q, comp_ref[:, kc]) + comp_bias, comp_ref, vc),
                (score(q, mem_ref[:, kc]) + mem_bias, mem_ref, vc),
            ]
            for o in own_refs[:-1]:
                pieces.append((score(q, o[:, kc]), o, vc))
            o = own_refs[-1]
            pieces.append((jnp.where(causal, score(q, o[:, kc]), NEG), o, vc))
            top, norm, mixed = gathered(pieces, None)
            mix_ref[:, kc] = mixed
            stats = jnp.where(lane == 2 * h, top, stats)
            stats = jnp.where(lane == 2 * h + 1, norm, stats)
        stat_ref[...] = stats

    outs = [((rows, width), F32), ((rows, 128), F32)]
    scratch = [pltpu.VMEM((n_comp, 2 * width), BF16)]
    return call(body, outs, [q, *own, memory, *early], scratch)


def gathered(pieces, so_far):
    top = None if so_far is None else so_far[0]
    for s, _, _ in pieces:
        m = jnp.max(s, axis=1, keepdims=True)
        top = m if top is None else jnp.maximum(top, m)
    norm = mixed = None
    if so_far is not None:
        shrink = jnp.exp2((so_far[0] - top) * SCALE)
        norm, mixed = so_far[1] * shrink, so_far[2] * shrink
    for s, v, cols in pieces:
        p = jnp.exp2((s - top) * SCALE)
        total = jnp.sum(p, axis=1, keepdims=True)
        part = jnp.dot(p.astype(BF16), v[:, cols], preferred_element_type=F32)
        norm = total if norm is None else norm + total
        mixed = part if mixed is None else mixed + part
    return top, norm, mixed


def attend_end(slots, q, begun, memory, heads_of, late, weight):
    rows, width = q.shape
    n = slots.rows
    n_comp = -(-(RATE * n + 16) // 128) * 128
    heads = width // DH

    def body(q_ref, mix_ref, stat_ref, mem_ref, *refs):
        early_refs = refs[:RATE]
        late_refs = refs[RATE : 2 * RATE]
        w_ref, out_ref, comp_ref = refs[2 * RATE :]
        seg = lax.axis_index("seg")
        weight = filter_rows(w_ref)
        for a in range(RATE):
            comp_ref[a * n : (a + 1) * n, :] = late_refs[a][...]
        pad = n_comp - RATE * n
        row = lax.broadcasted_iota(jnp.int32, (pad, 1), 0)
        extra = jnp.zeros((pad, 2 * width), F32)
        for k, b in enumerate(slots.joints):
            at = slots.late[b]
            tail = late_refs[b][...].astype(F32)
            parts = [tail[at + i : at + i + 1] for i in range(slots.tail[b])]
            at = slots.early[b + 1]
            head = early_refs[b + 1][...].astype(F32)
            parts += [head[at + i : at + i + 1] for i in range(slots.offset[b + 1])]
            slot = sum(p * weight[r] for r, p in enumerate(parts))
            extra = jnp.where(row == k, slot, extra)
        comp_ref[RATE * n :, :] = extra.astype(BF16)
        spans = [(a * n, slots.late[a]) for a in range(RATE)] + [(RATE * n, len(slots.joints))]
        comp_bias = slot_bias(seg, n_comp, spans)
        mem_bias = jnp.where(seg >= 1, 0.0, NEG).astype(F32)
        for h in range(heads):
            kc = slice(h * DH, (h + 1) * DH)
            vc = slice(width + h * DH, width + (h + 1) * DH)
            q = q_ref[:, kc]
            pieces = [
                (score(q, comp_ref[:, kc]) + comp_bias, comp_ref, vc),
                (score(q, mem_ref[:, kc]) + mem_bias, mem_ref, vc),
            ]
            so_far = (
                stat_ref[:, 2 * h : 2 * h + 1],
                stat_ref[:, 2 * h + 1 : 2 * h + 2],
                mix_ref[:, kc],
            )
            _, norm, mixed = gathered(pieces, so_far)
            out_ref[:, kc] = (mixed / norm).astype(BF16)

    outs = [((rows, width), BF16)]
    scratch = [pltpu.VMEM((n_comp, 2 * width), BF16)]
    args = [q, *begun, memory, *heads_of, *late, weight]
    return call(body, outs, args, scratch)[0]


def output_begin(ctx, w_full, xored):
    rows = ctx[0].shape[0]

    def body(*refs):
        w_ref, acc_ref = refs[len(ctx) :]
        acc_ref[...] = output_sum(refs[: len(ctx)], range(len(ctx)), w_ref, xored)

    outs = [((rows, w_full.shape[1]), F32)]
    return call(body, outs, [*ctx, w_full])[0]


def output_sum(ctx, steps, w_ref, xored):
    width = ctx[0].shape[1]
    unit = xored or width
    size = w_ref.shape[0] // width
    acc = None
    for t, c in zip(steps, ctx):
        for k in range(width // unit):
            block = source_of(t, OUT_RING(size)) * (width // unit) + k
            if xored:
                block = lax.bitwise_xor(block, lax.axis_index("seg"))
            start = pl.multiple_of(block * unit, unit)
            part = jnp.dot(
                c[:, k * unit : (k + 1) * unit],
                w_ref[pl.ds(start, unit), :],
                preferred_element_type=F32,
            )
            acc = part if acc is None else acc + part
    return acc


def output_end(offset, n_rows, last_step, ctx, begun, w_full, xored, result):
    rows = ctx.shape[0]
    columns = w_full.shape[1]
    n_extra = 1 if result is not None else 0
    n_copy = 4 if rows % 64 == 0 else 1
    part = rows // n_copy

    def body(ctx_ref, acc_ref, w_ref, *refs):
        out_ref, held, sems = refs[n_extra:]
        acc = output_sum([ctx_ref], [last_step], w_ref, xored)
        copies = []
        for k in range(n_copy):
            at = pl.ds(k * part, part)
            held[at, :] = (acc_ref[at, :] + acc[k * part : (k + 1) * part]).astype(BF16)
            to = out_ref.at[pl.ds(offset + k * part, part), :]
            copies.append(pltpu.make_async_copy(held.at[at, :], to, sems.at[k]))
            copies[-1].start()
        for copy in copies:
            copy.wait()

    args = [ctx, begun, w_full]
    in_specs = [vmem(), vmem(), vmem()]
    aliases = {}
    if result is not None:
        args.append(result)
        in_specs.append(hbm())
        aliases = {3: 0}
    return pl.pallas_call(
        body,
        out_shape=jax.ShapeDtypeStruct((n_rows, columns), BF16),
        in_specs=in_specs,
        out_specs=hbm(),
        scratch_shapes=[pltpu.VMEM((rows, columns), BF16), pltpu.SemaphoreType.DMA((n_copy,))],
        input_output_aliases=aliases,
        compiler_params=params(),
    )(*args)


def gather_rows(block, by_xor):
    size = lax.axis_size("seg")
    if size & (size - 1):
        return lax.all_gather(block, "seg", axis=0, tiled=True)
    seg = lax.axis_index("seg")
    step = 1
    while step < size:
        other = lax.ppermute(block, "seg", [(i, i ^ step) for i in range(size)])
        if by_xor:
            block = join(block, other)
        else:
            upper = (seg // step) % 2 == 1
            low = jnp.where(upper, other, block)
            high = jnp.where(upper, block, other)
            block = jnp.concatenate([low, high], axis=0)
        step *= 2
    return block


def local(layer_input, w_qkv, comp_weight, w_out):
    n_head = lax.axis_size("head")
    seg_len = layer_input.shape[1]
    rows = pltpu.with_memory_space_constraint(layer_input[0], pltpu.HBM)
    w3 = pltpu.with_memory_space_constraint(jnp.transpose(w_qkv, (1, 0, 2)), pltpu.HBM)
    width = w_qkv.shape[2]
    weight = comp_weight

    early_rows = seg_len * EARLY // 16
    early_piece, late_piece = early_rows // EARLY_PARTS, (seg_len - early_rows) // LATE_PARTS
    slots = Slots(seg_len, early_rows)
    starts = [c * early_piece for c in range(EARLY_PARTS)]
    first = [[chunk] for chunk in split(rows, starts, early_piece)]
    starts = [early_rows + c * late_piece for c in range(LATE_PARTS)]
    second = [[chunk] for chunk in split(rows, starts, late_piece)]
    n_seg = lax.axis_size("seg")
    in_ring, out_ring = IN_RING(n_head), OUT_RING(n_head)
    own_rows = w_out.shape[0]
    power = n_seg & (n_seg - 1) == 0
    xored = own_rows if power and own_rows % DH == 0 and width % own_rows == 0 else 0

    w_vmem, col_sums = fetch_weights(w3)
    for _ in range(1, n_head):
        for chunk in first:
            chunk.append(around(chunk[-1], in_ring))
    w_full = gather_rows(w_out, xored)
    q0, kv0 = project(first, w_vmem, col_sums)
    early_parts = compress(slots, [kv0], weight)
    mem0 = passed_along(kv0, 1)
    early = [passed_along(p, BACK - a) for a, p in enumerate(early_parts)]

    for _ in range(1, n_head):
        for chunk in second:
            chunk.append(around(chunk[-1], in_ring))
    begun = project_begin([chunk[:-1] for chunk in second], w_vmem)
    lasts = [chunk[-1] for chunk in second]
    kv1 = project_end(lasts, begun, w_vmem, col_sums, (1, 2))
    mem1 = passed_along(kv1, 1)
    late_parts = compress(slots, [kv0, kv1], weight)
    late = [passed_along(p, BACK - a) for a, p in enumerate(late_parts)]
    q1 = project_end(lasts, begun, w_vmem, col_sums, (0,))

    rings = []
    for q, own in ((q0, [kv0]), (q1, [kv0, kv1])):
        part = attend_begin(slots, q, own, mem0, early)
        ctx = attend_end(slots, q, part, mem1, early, late, weight)
        rings.append([ctx])
    for _ in range(1, n_head):
        for ring in rings:
            ring.append(around(ring[-1], out_ring))
    result = None
    for h, ring in enumerate(rings):
        part = output_begin(ring[:-1], w_full, xored)
        result = output_end(
            h * early_rows, seg_len, n_head - 1, ring[-1], part, w_full, xored, result,
        )
    return result[None]


def solution(mesh):
    return jax.shard_map(
        local,
        mesh=mesh,
        in_specs=(
            P(None, "seg", "head"),
            P(None, None, "head"),
            P(None, None, "head"),
            P("seg", "head"),
        ),
        out_specs=P(None, "seg", "head"),
        check_vma=False,
    )
```

```python
import math

import jax
import jax.numpy as jnp
from jax import lax
from jax.experimental import pallas as pl
from jax.experimental.pallas import tpu as pltpu
from jax.sharding import PartitionSpec as P


DH = 128
RATE = 3
BACK = 4
BF16 = jnp.bfloat16
F32 = jnp.float32
NEG = -1e30
VMEM_LIMIT = 14 * 1024 * 1024


def params():
    return pltpu.CompilerParams(vmem_limit_bytes=VMEM_LIMIT)


def vmem():
    return pl.BlockSpec(memory_space=pltpu.VMEM)


def ring_of(size):
    ups = [i for i in range(size) if i % 2 == 1]
    downs = [i for i in range(size) if i % 2 == 0 and i > 0]
    return [0] + ups + downs[::-1]


def offset_of(step):
    return -((step + 1) // 2) if step % 2 else step // 2


EARLY = 8
FINAL = 2
EARLY_PARTS, LATE_PARTS = 2, 2


def spread(held, step):
    order = ring_of(lax.axis_size("head"))
    towards = order[1:] + order[:1]
    if step % 2 == 0:
        order, towards = towards, order
    block = held[0] if step <= 2 else held[step - 2]
    return lax.ppermute(block, "head", list(zip(order, towards)))


def passed_along(block, distance):
    size = lax.axis_size("seg")
    route = [(i, (i + distance) % size) for i in range(size)]
    return lax.ppermute(block, "seg", route)


def source_of(step, size):
    order = ring_of(size)
    z = lax.axis_index("head")
    found = jnp.int32(0)
    for here in range(size):
        at = (order.index(here) + offset_of(step)) % size
        found = jnp.where(z == here, order[at], found)
    return found


def hbm():
    return pl.BlockSpec(memory_space=pltpu.HBM)


def call(body, outs, args, scratch=(), in_specs=None):
    return pl.pallas_call(
        body,
        out_shape=tuple(jax.ShapeDtypeStruct(s, d) for s, d in outs),
        in_specs=in_specs or [vmem()] * len(args),
        out_specs=tuple(vmem() for _ in outs),
        scratch_shapes=list(scratch),
        compiler_params=params(),
    )(*args)


def split(rows, starts, piece):
    def body(src, *refs):
        sems = refs[-1]
        copies = [
            pltpu.make_async_copy(src.at[pl.ds(at, piece), :], out, sems.at[i])
            for i, (at, out) in enumerate(zip(starts, refs))
        ]
        for copy in copies:
            copy.start()
        for copy in copies:
            copy.wait()

    outs = [((piece, rows.shape[1]), rows.dtype)] * len(starts)
    scratch = [pltpu.SemaphoreType.DMA((len(starts),))]
    return call(body, outs, [rows], scratch, [hbm()])


def join(one, two):
    n = one.shape[0]

    def body(one_ref, two_ref, out_ref):
        out_ref[:n, :] = one_ref[...]
        out_ref[n:, :] = two_ref[...]

    return call(body, [((2 * n, one.shape[1]), one.dtype)], [one, two])[0]


def weight_rows(w_ref, i, source, feats):
    start = pl.multiple_of(source * feats, feats)
    return w_ref[i, pl.ds(start, feats), :]


def moments(block):
    x = block.astype(F32)
    total = jnp.sum(x, axis=1, keepdims=True)
    off = x - total / x.shape[1]
    return total, jnp.sum(off * off, axis=1, keepdims=True)


def joined_moments(parts, feats):
    count = feats * len(parts)
    mean = sum(t for t, _ in parts) / count
    square = sum(q + feats * jnp.square(t / feats - mean) for t, q in parts)
    return mean, lax.rsqrt(square / count + 1e-05)


def project_sum(blocks, steps, w_ref, i):
    feats = blocks[0].shape[1]
    size = w_ref.shape[1] // feats
    acc = None
    for t, block in zip(steps, blocks):
        part = jnp.dot(
            block[...], weight_rows(w_ref, i, source_of(t, size), feats), preferred_element_type=F32
        )
        acc = part if acc is None else acc + part
    return acc


def fetch_weights(w3):
    n_kind, _, width = w3.shape

    def body(src, w_ref, sum_ref, sems):
        copies = [
            pltpu.make_async_copy(src.at[i], w_ref.at[i], sems.at[i]) for i in range(n_kind)
        ]
        for copy in copies:
            copy.start()
        for i, copy in enumerate(copies):
            copy.wait()
            total = jnp.sum(w_ref[i].astype(F32), axis=0, keepdims=True)
            sum_ref[:, i * width : (i + 1) * width] = jnp.broadcast_to(total, (8, width))

    return pl.pallas_call(
        body,
        out_shape=(
            jax.ShapeDtypeStruct(w3.shape, w3.dtype),
            jax.ShapeDtypeStruct((8, n_kind * width), F32),
        ),
        in_specs=[hbm()],
        out_specs=(vmem(), vmem()),
        scratch_shapes=[pltpu.SemaphoreType.DMA((n_kind,))],
        compiler_params=params(),
        name="fetch",
    )(w3)


def project(chunks, w3, col_sums):
    n_head, n_chunk = len(chunks[0]), len(chunks)
    piece, feats = chunks[0][0].shape
    width = w3.shape[2]
    rows = piece * n_chunk

    def body(*refs):
        w_ref, sum_ref, q_ref, kv_ref = refs[n_head * n_chunk :]
        for c in range(n_chunk):
            blocks = refs[c * n_head : (c + 1) * n_head]
            mean, inv = joined_moments([moments(b[...]) for b in blocks], feats)
            at = pl.ds(c * piece, piece)
            for i in range(3):
                acc = project_sum(blocks, range(n_head), w_ref, i)
                cols = slice(i * width, (i + 1) * width)
                acc = ((acc - mean * sum_ref[0:1, cols]) * inv).astype(BF16)
                if i == 0:
                    q_ref[at, :] = acc
                else:
                    kv_ref[at, (i - 1) * width : i * width] = acc

    flat = [b for chunk in chunks for b in chunk]
    outs = [((rows, width), BF16), ((rows, 2 * width), BF16)]
    return call(body, outs, [*flat, w3, col_sums])


def project_begin(chunks, steps, w3):
    n_here, n_chunk = len(chunks[0]), len(chunks)
    piece, _ = chunks[0][0].shape
    width = w3.shape[2]

    def body(*refs):
        w_ref, acc_ref, mom_ref = refs[n_here * n_chunk :]
        lane = lax.broadcasted_iota(jnp.int32, (piece, 128), 1)
        for c in range(n_chunk):
            blocks = refs[c * n_here : (c + 1) * n_here]
            at = pl.ds(c * piece, piece)
            for i in range(3):
                acc_ref[at, i * width : (i + 1) * width] = project_sum(
                    blocks, steps, w_ref, i
                )
            held = jnp.zeros((piece, 128), F32)
            for t, block in enumerate(blocks):
                for k, value in enumerate(moments(block[...])):
                    held = jnp.where(lane == 2 * t + k, value, held)
            mom_ref[at, :] = held

    flat = [b for chunk in chunks for b in chunk]
    outs = [((piece * n_chunk, 3 * width), F32), ((piece * n_chunk, 128), F32)]
    return call(body, outs, [*flat, w3])


def project_end(lasts, last, begun, w3, col_sums, kinds):
    n_chunk = len(lasts)
    piece, feats = lasts[0].shape
    width = w3.shape[2]
    rows = piece * n_chunk
    n_begun = w3.shape[1] // feats - 1

    def body(*refs):
        w_ref, acc_ref, mom_ref, sum_ref, out_ref = refs[n_chunk:]
        for c in range(n_chunk):
            at = pl.ds(c * piece, piece)
            held = mom_ref[at, :]
            parts = [(held[:, 2 * t : 2 * t + 1], held[:, 2 * t + 1 : 2 * t + 2]) for t in range(n_begun)]
            parts.append(moments(refs[c][...]))
            mean, inv = joined_moments(parts, feats)
            for k, i in enumerate(kinds):
                cols = slice(i * width, (i + 1) * width)
                acc = acc_ref[at, cols] + project_sum([refs[c]], [last], w_ref, i)
                acc = (acc - mean * sum_ref[0:1, cols]) * inv
                out_ref[at, k * width : (k + 1) * width] = acc.astype(BF16)

    outs = [((rows, len(kinds) * width), BF16)]
    return call(body, outs, [*lasts, w3, *begun, col_sums])[0]


class Slots:
    def __init__(self, seg_len, early_rows):
        self.seg_len, self.early_rows = seg_len, early_rows
        self.offset = [(-a * seg_len) % RATE for a in range(RATE)]
        self.count = [(seg_len - o) // RATE for o in self.offset]
        self.tail = [seg_len - o - RATE * n for o, n in zip(self.offset, self.count)]
        self.early = [max(0, (early_rows - o) // RATE) for o in self.offset]
        self.late = [n - e for n, e in zip(self.count, self.early)]
        most = max(
            max(e + o for e, o in zip(self.early, self.offset)),
            max(l + t for l, t in zip(self.late, self.tail)),
        )
        self.rows = -(-most // 8) * 8
        self.pitch = -(-most // 16) * 16
        self.joints = [b for b in range(RATE - 1) if self.tail[b] > 0]


def filter_rows(w_ref):
    return [
        jnp.concatenate([w_ref[r, k : k + 1, :].astype(F32) for k in range(2)], axis=1)
        for r in range(RATE)
    ]


def write_slots(slots, late, sources, w_ref, outs):
    weight = filter_rows(w_ref)
    n = slots.rows
    main = sources[-1]
    base = slots.early_rows if late else 0
    counts = slots.late if late else slots.early
    begins = slots.early if late else [0] * RATE
    firsts = [slots.offset[a] + RATE * begins[a] for a in range(RATE)]
    wanted = sorted({f + r for f in firsts for r in range(RATE)})

    def hits(first, rows, at):
        row = lax.broadcasted_iota(jnp.int32, (n, rows), 0)
        col = lax.broadcasted_iota(jnp.int32, (n, rows), 1) + at
        return jnp.where(col == first + RATE * row, 1.0, 0.0)

    chosen = jnp.concatenate([hits(f, main.shape[0], base) for f in wanted], axis=0).astype(BF16)
    picks = jnp.dot(chosen, main[...], preferred_element_type=F32)
    row = lax.broadcasted_iota(jnp.int32, (n, 1), 0)
    picked = {}
    for k, f in enumerate(wanted):
        got = picks[k * n : (k + 1) * n]
        if f < base:
            back = base - f
            got = jnp.where(row == 0, sources[0][-16:, :].astype(F32)[16 - back : 17 - back], got)
        picked[f] = got
    raw = main[...].astype(F32)
    for a in range(RATE):
        acc = None
        for r in range(RATE):
            term = picked[firsts[a] + r] * weight[r]
            acc = term if acc is None else acc + term
        n_raw = slots.tail[a] if late else slots.offset[a]
        for i in range(n_raw):
            at = main.shape[0] - n_raw + i if late else i
            acc = jnp.where(row == counts[a] + i, raw[at : at + 1, :], acc)
        outs[a][...] = acc.astype(BF16)


def compress(slots, sources, weight):
    n_in = len(sources)

    def body(*refs):
        write_slots(slots, n_in == 2, refs[:n_in], refs[n_in], refs[n_in + 1 :])

    outs = [((slots.rows, 2 * weight.shape[2]), BF16)] * RATE
    return call(body, outs, [*sources, weight])


SCALE = math.log2(math.e) / math.sqrt(DH)


def score(q, keys):
    return lax.dot_general(q, keys, (((1,), (1,)), ((), ())), preferred_element_type=F32)


def slot_bias(seg, n_cols, spans):
    col = lax.broadcasted_iota(jnp.int32, (1, n_cols), 1)
    valid = col < 0
    for begin, count in spans:
        valid |= (col >= begin) & (col < begin + count)
    return jnp.where(valid & (seg >= BACK), 0.0, NEG).astype(F32)


def attend_begin(slots, q, own, memory, early):
    rows, width = q.shape
    n, pitch = slots.rows, slots.pitch
    n_comp = -(-RATE * pitch // 128) * 128
    heads = width // DH

    def body(q_ref, *refs):
        own_refs = refs[: len(own)]
        mem_ref = refs[len(own)]
        early_refs = refs[len(own) + 1 : len(own) + 1 + RATE]
        mix_ref, stat_ref, comp_ref = refs[len(own) + 1 + RATE :]
        seg = lax.axis_index("seg")
        comp_ref[...] = jnp.zeros((n_comp, 2 * width), BF16)
        for a in range(RATE):
            comp_ref[a * pitch : a * pitch + n, :] = early_refs[a][...]
        comp_bias = slot_bias(seg, n_comp, [(a * pitch, slots.early[a]) for a in range(RATE)])
        mem_bias = jnp.where(seg >= 1, 0.0, NEG).astype(F32)
        q_row = lax.broadcasted_iota(jnp.int32, (rows, rows), 0)
        k_row = lax.broadcasted_iota(jnp.int32, (rows, rows), 1)
        causal = k_row <= q_row
        lane = lax.broadcasted_iota(jnp.int32, (rows, 128), 1)
        stats = jnp.zeros((rows, 128), F32)
        for h in range(heads):
            kc = slice(h * DH, (h + 1) * DH)
            vc = slice(width + h * DH, width + (h + 1) * DH)
            q = q_ref[:, kc]
            pieces = [
                (score(q, comp_ref[:, kc]) + comp_bias, comp_ref, vc),
                (score(q, mem_ref[:, kc]) + mem_bias, mem_ref, vc),
            ]
            for o in own_refs[:-1]:
                pieces.append((score(q, o[:, kc]), o, vc))
            o = own_refs[-1]
            pieces.append((jnp.where(causal, score(q, o[:, kc]), NEG), o, vc))
            top, norm, mixed = gathered(pieces, None)
            mix_ref[:, kc] = mixed
            stats = jnp.where(lane == 2 * h, top, stats)
            stats = jnp.where(lane == 2 * h + 1, norm, stats)
        stat_ref[...] = stats

    outs = [((rows, width), F32), ((rows, 128), F32)]
    scratch = [pltpu.VMEM((n_comp, 2 * width), BF16)]
    return call(body, outs, [q, *own, memory, *early], scratch)


def gathered(pieces, so_far):
    top = None if so_far is None else so_far[0]
    for s, _, _ in pieces:
        m = jnp.max(s, axis=1, keepdims=True)
        top = m if top is None else jnp.maximum(top, m)
    norm = mixed = None
    if so_far is not None:
        shrink = jnp.exp2((so_far[0] - top) * SCALE)
        norm, mixed = so_far[1] * shrink, so_far[2] * shrink
    for s, v, cols in pieces:
        p = jnp.exp2((s - top) * SCALE)
        total = jnp.sum(p, axis=1, keepdims=True)
        part = jnp.dot(p.astype(BF16), v[:, cols], preferred_element_type=F32)
        norm = total if norm is None else norm + total
        mixed = part if mixed is None else mixed + part
    return top, norm, mixed


def state_of(mix_ref, stat_ref, h):
    top, norm = (stat_ref[:, 2 * h + k : 2 * h + k + 1] for k in range(2))
    return top, norm, mix_ref[:, h * DH : (h + 1) * DH]


def attend_more(q, begun, memory):
    rows, width = q.shape

    def body(q_ref, mix_ref, stat_ref, mem_ref, mix_out, stat_out):
        seg = lax.axis_index("seg")
        mem_bias = jnp.where(seg >= 1, 0.0, NEG).astype(F32)
        lane = lax.broadcasted_iota(jnp.int32, (rows, 128), 1)
        stats = jnp.zeros((rows, 128), F32)
        for h in range(width // DH):
            kc = slice(h * DH, (h + 1) * DH)
            vc = slice(width + h * DH, width + (h + 1) * DH)
            pieces = [(score(q_ref[:, kc], mem_ref[:, kc]) + mem_bias, mem_ref, vc)]
            top, norm, mixed = gathered(pieces, state_of(mix_ref, stat_ref, h))
            mix_out[:, kc] = mixed
            stats = jnp.where(lane == 2 * h, top, stats)
            stats = jnp.where(lane == 2 * h + 1, norm, stats)
        stat_out[...] = stats

    outs = [((rows, width), F32), ((rows, 128), F32)]
    return call(body, outs, [q, *begun, memory])


def attend_end(slots, q, begun, heads_of, late, weight):
    rows, width = q.shape
    n, pitch = slots.rows, slots.pitch
    n_comp = -(-(RATE * pitch + 16) // 128) * 128
    heads = width // DH

    def body(q_ref, mix_ref, stat_ref, *refs):
        early_refs = refs[:RATE]
        late_refs = refs[RATE : 2 * RATE]
        w_ref, out_ref, comp_ref = refs[2 * RATE :]
        seg = lax.axis_index("seg")
        weight = filter_rows(w_ref)
        if n < pitch:
            comp_ref[: RATE * pitch, :] = jnp.zeros((RATE * pitch, 2 * width), BF16)
        for a in range(RATE):
            comp_ref[a * pitch : a * pitch + n, :] = late_refs[a][...]
        pad = n_comp - RATE * pitch
        row = lax.broadcasted_iota(jnp.int32, (pad, 1), 0)
        extra = jnp.zeros((pad, 2 * width), F32)
        for k, b in enumerate(slots.joints):
            at = slots.late[b]
            tail = late_refs[b][...].astype(F32)
            parts = [tail[at + i : at + i + 1] for i in range(slots.tail[b])]
            at = slots.early[b + 1]
            head = early_refs[b + 1][...].astype(F32)
            parts += [head[at + i : at + i + 1] for i in range(slots.offset[b + 1])]
            slot = sum(p * weight[r] for r, p in enumerate(parts))
            extra = jnp.where(row == k, slot, extra)
        comp_ref[RATE * pitch :, :] = extra.astype(BF16)
        spans = [(a * pitch, slots.late[a]) for a in range(RATE)]
        spans.append((RATE * pitch, len(slots.joints)))
        comp_bias = slot_bias(seg, n_comp, spans)
        for h in range(heads):
            kc = slice(h * DH, (h + 1) * DH)
            vc = slice(width + h * DH, width + (h + 1) * DH)
            pieces = [(score(q_ref[:, kc], comp_ref[:, kc]) + comp_bias, comp_ref, vc)]
            _, norm, mixed = gathered(pieces, state_of(mix_ref, stat_ref, h))
            out_ref[:, kc] = (mixed / norm).astype(BF16)

    outs = [((rows, width), BF16)]
    scratch = [pltpu.VMEM((n_comp, 2 * width), BF16)]
    args = [q, *begun, *heads_of, *late, weight]
    return call(body, outs, args, scratch)[0]


def output_begin(ctx, steps, w_full, xored):
    rows = ctx[0].shape[0]

    def body(*refs):
        w_ref, acc_ref = refs[len(ctx) :]
        acc_ref[...] = output_sum(refs[: len(ctx)], steps, w_ref, xored)

    outs = [((rows, w_full.shape[1]), F32)]
    return call(body, outs, [*ctx, w_full])[0]


def output_sum(ctx, steps, w_ref, xored):
    width = ctx[0].shape[1]
    unit = xored or width
    size = w_ref.shape[0] // width
    acc = None
    for t, c in zip(steps, ctx):
        for k in range(width // unit):
            block = source_of(t, size) * (width // unit) + k
            if xored:
                block = lax.bitwise_xor(block, lax.axis_index("seg"))
            start = pl.multiple_of(block * unit, unit)
            part = jnp.dot(
                c[:, k * unit : (k + 1) * unit],
                w_ref[pl.ds(start, unit), :],
                preferred_element_type=F32,
            )
            acc = part if acc is None else acc + part
    return acc


def output_end(offset, n_rows, last_step, ctx, begun, w_full, xored, result):
    rows = ctx.shape[0]
    columns = w_full.shape[1]
    n_extra = 1 if result is not None else 0
    n_copy = 4 if rows % 64 == 0 else 1
    part = rows // n_copy

    def body(ctx_ref, acc_ref, w_ref, *refs):
        out_ref, held, sems = refs[n_extra:]
        acc = output_sum([ctx_ref], [last_step], w_ref, xored)
        copies = []
        for k in range(n_copy):
            at = pl.ds(k * part, part)
            held[at, :] = (acc_ref[at, :] + acc[k * part : (k + 1) * part]).astype(BF16)
            to = out_ref.at[pl.ds(offset + k * part, part), :]
            copies.append(pltpu.make_async_copy(held.at[at, :], to, sems.at[k]))
            copies[-1].start()
        for copy in copies:
            copy.wait()

    args = [ctx, begun, w_full]
    in_specs = [vmem(), vmem(), vmem()]
    aliases = {}
    if result is not None:
        args.append(result)
        in_specs.append(hbm())
        aliases = {3: 0}
    return pl.pallas_call(
        body,
        out_shape=jax.ShapeDtypeStruct((n_rows, columns), BF16),
        in_specs=in_specs,
        out_specs=hbm(),
        scratch_shapes=[pltpu.VMEM((rows, columns), BF16), pltpu.SemaphoreType.DMA((n_copy,))],
        input_output_aliases=aliases,
        compiler_params=params(),
    )(*args)


def gather_rows(block, by_xor):
    size = lax.axis_size("seg")
    if size & (size - 1):
        return lax.all_gather(block, "seg", axis=0, tiled=True)
    seg = lax.axis_index("seg")
    step = 1
    while step < size:
        other = lax.ppermute(block, "seg", [(i, i ^ step) for i in range(size)])
        if by_xor:
            block = join(block, other)
        else:
            upper = (seg // step) % 2 == 1
            low = jnp.where(upper, other, block)
            high = jnp.where(upper, block, other)
            block = jnp.concatenate([low, high], axis=0)
        step *= 2
    return block


def local(layer_input, w_qkv, comp_weight, w_out):
    n_head = lax.axis_size("head")
    seg_len = layer_input.shape[1]
    rows = pltpu.with_memory_space_constraint(layer_input[0], pltpu.HBM)
    w3 = pltpu.with_memory_space_constraint(jnp.transpose(w_qkv, (1, 0, 2)), pltpu.HBM)
    width = w_qkv.shape[2]
    weight = comp_weight

    early_rows = seg_len * EARLY // 16
    early_piece, late_piece = early_rows // EARLY_PARTS, (seg_len - early_rows) // LATE_PARTS
    slots = Slots(seg_len, early_rows)
    starts = [c * early_piece for c in range(EARLY_PARTS)]
    first = [[chunk] for chunk in split(rows, starts, early_piece)]
    starts = [early_rows + c * late_piece for c in range(LATE_PARTS)]
    second = [[chunk] for chunk in split(rows, starts, late_piece)]
    n_seg = lax.axis_size("seg")
    own_rows = w_out.shape[0]
    power = n_seg & (n_seg - 1) == 0
    xored = own_rows if power and own_rows % DH == 0 and width % own_rows == 0 else 0

    w_vmem, col_sums = fetch_weights(w3)
    for t in range(1, n_head):
        for chunk in first:
            chunk.append(spread(chunk, t))
    w_full = gather_rows(w_out, xored)
    q0, kv0 = project(first, w_vmem, col_sums)
    early_parts = compress(slots, [kv0], weight)
    mem0 = passed_along(kv0, 1)
    early = [passed_along(p, BACK - a) for a, p in enumerate(early_parts)]

    for t in range(1, n_head):
        for chunk in second:
            chunk.append(spread(chunk, t))
    final = min(FINAL, n_head - 1)
    steps = [t for t in range(n_head) if t != final]
    begun = project_begin([[chunk[t] for t in steps] for chunk in second], steps, w_vmem)
    lasts = [chunk[final] for chunk in second]
    kv1 = project_end(lasts, final, begun, w_vmem, col_sums, (1, 2))
    mem1 = passed_along(kv1, 1)
    late_parts = compress(slots, [kv0, kv1], weight)
    late = [passed_along(p, BACK - a) for a, p in enumerate(late_parts)]
    q1 = project_end(lasts, final, begun, w_vmem, col_sums, (0,))

    rings = []
    for q, own in ((q0, [kv0]), (q1, [kv0, kv1])):
        part = attend_begin(slots, q, own, mem0, early)
        part = attend_more(q, part, mem1)
        ctx = attend_end(slots, q, part, early, late, weight)
        rings.append([ctx])
    for t in range(1, n_head):
        for ring in rings:
            ring.append(spread(ring, t))
    result = None
    for h, ring in enumerate(rings):
        part = output_begin([ring[t] for t in steps], steps, w_full, xored)
        result = output_end(
            h * early_rows, seg_len, final, ring[final], part, w_full, xored, result,
        )
    return result[None]


def solution(mesh):
    return jax.shard_map(
        local,
        mesh=mesh,
        in_specs=(
            P(None, "seg", "head"),
            P(None, None, "head"),
            P(None, None, "head"),
            P("seg", "head"),
        ),
        out_specs=P(None, "seg", "head"),
        check_vma=False,
    )
```

```python
import math

import jax
import jax.numpy as jnp
from jax import lax
from jax.experimental import pallas as pl
from jax.experimental.pallas import tpu as pltpu
from jax.sharding import PartitionSpec as P


DH = 128
RATE = 3
BACK = 4
BF16 = jnp.bfloat16
F32 = jnp.float32
NEG = -1e30
VMEM_LIMIT = 14 * 1024 * 1024


def params():
    return pltpu.CompilerParams(vmem_limit_bytes=VMEM_LIMIT)


def vmem():
    return pl.BlockSpec(memory_space=pltpu.VMEM)


def ring_of(size):
    ups = [i for i in range(size) if i % 2 == 1]
    downs = [i for i in range(size) if i % 2 == 0 and i > 0]
    return [0] + ups + downs[::-1]


def offset_of(step):
    return -((step + 1) // 2) if step % 2 else step // 2


EARLY = 10
FINAL = 2
EARLY_PARTS, LATE_PARTS = 2, 2


def spread(held, step):
    order = ring_of(lax.axis_size("head"))
    towards = order[1:] + order[:1]
    if step % 2 == 0:
        order, towards = towards, order
    block = held[0] if step <= 2 else held[step - 2]
    return lax.ppermute(block, "head", list(zip(order, towards)))


def passed_along(block, distance):
    size = lax.axis_size("seg")
    route = [(i, (i + distance) % size) for i in range(size)]
    return lax.ppermute(block, "seg", route)


def source_of(step, size):
    order = ring_of(size)
    z = lax.axis_index("head")
    found = jnp.int32(0)
    for here in range(size):
        at = (order.index(here) + offset_of(step)) % size
        found = jnp.where(z == here, order[at], found)
    return found


def hbm():
    return pl.BlockSpec(memory_space=pltpu.HBM)


def call(body, outs, args, scratch=(), in_specs=None):
    return pl.pallas_call(
        body,
        out_shape=tuple(jax.ShapeDtypeStruct(s, d) for s, d in outs),
        in_specs=in_specs or [vmem()] * len(args),
        out_specs=tuple(vmem() for _ in outs),
        scratch_shapes=list(scratch),
        compiler_params=params(),
    )(*args)


def split(rows, starts, piece):
    def body(src, *refs):
        sems = refs[-1]
        copies = [
            pltpu.make_async_copy(src.at[pl.ds(at, piece), :], out, sems.at[i])
            for i, (at, out) in enumerate(zip(starts, refs))
        ]
        for copy in copies:
            copy.start()
        for copy in copies:
            copy.wait()

    outs = [((piece, rows.shape[1]), rows.dtype)] * len(starts)
    scratch = [pltpu.SemaphoreType.DMA((len(starts),))]
    return call(body, outs, [rows], scratch, [hbm()])


def join(one, two):
    n = one.shape[0]

    def body(one_ref, two_ref, out_ref):
        out_ref[:n, :] = one_ref[...]
        out_ref[n:, :] = two_ref[...]

    return call(body, [((2 * n, one.shape[1]), one.dtype)], [one, two])[0]


def weight_rows(w_ref, i, source, feats):
    start = pl.multiple_of(source * feats, feats)
    return w_ref[i, pl.ds(start, feats), :]


def moments(block):
    x = block.astype(F32)
    total = jnp.sum(x, axis=1, keepdims=True)
    off = x - total / x.shape[1]
    return total, jnp.sum(off * off, axis=1, keepdims=True)


def joined_moments(parts, feats):
    count = feats * len(parts)
    mean = sum(t for t, _ in parts) / count
    square = sum(q + feats * jnp.square(t / feats - mean) for t, q in parts)
    return mean, lax.rsqrt(square / count + 1e-05)


def project_sum(blocks, steps, w_ref, i):
    feats = blocks[0].shape[1]
    size = w_ref.shape[1] // feats
    acc = None
    for t, block in zip(steps, blocks):
        part = jnp.dot(
            block[...], weight_rows(w_ref, i, source_of(t, size), feats), preferred_element_type=F32
        )
        acc = part if acc is None else acc + part
    return acc


def fetch_weights(w3):
    n_kind, _, width = w3.shape

    def body(src, w_ref, sum_ref, sems):
        copies = [
            pltpu.make_async_copy(src.at[i], w_ref.at[i], sems.at[i]) for i in range(n_kind)
        ]
        for copy in copies:
            copy.start()
        for i, copy in enumerate(copies):
            copy.wait()
            total = jnp.sum(w_ref[i].astype(F32), axis=0, keepdims=True)
            sum_ref[:, i * width : (i + 1) * width] = jnp.broadcast_to(total, (8, width))

    return pl.pallas_call(
        body,
        out_shape=(
            jax.ShapeDtypeStruct(w3.shape, w3.dtype),
            jax.ShapeDtypeStruct((8, n_kind * width), F32),
        ),
        in_specs=[hbm()],
        out_specs=(vmem(), vmem()),
        scratch_shapes=[pltpu.SemaphoreType.DMA((n_kind,))],
        compiler_params=params(),
        name="fetch",
    )(w3)


def project(chunks, w3, col_sums, q_rows):
    n_head, n_chunk = len(chunks[0]), len(chunks)
    piece, feats = chunks[0][0].shape
    width = w3.shape[2]
    rows = piece * n_chunk
    n_q = 2 if rows > q_rows else 1

    def body(*refs):
        w_ref, sum_ref, *q_refs, kv_ref = refs[n_head * n_chunk :]
        for c in range(n_chunk):
            blocks = refs[c * n_head : (c + 1) * n_head]
            mean, inv = joined_moments([moments(b[...]) for b in blocks], feats)
            begin, end = c * piece, (c + 1) * piece
            for i in range(3):
                acc = project_sum(blocks, range(n_head), w_ref, i)
                cols = slice(i * width, (i + 1) * width)
                acc = ((acc - mean * sum_ref[0:1, cols]) * inv).astype(BF16)
                if i > 0:
                    kv_ref[begin:end, (i - 1) * width : i * width] = acc
                    continue
                cut = min(max(q_rows - begin, 0), piece)
                if cut:
                    q_refs[0][begin : begin + cut, :] = acc[:cut]
                if cut < piece:
                    q_refs[1][begin + cut - q_rows : end - q_rows, :] = acc[cut:]

    flat = [b for chunk in chunks for b in chunk]
    outs = [((min(q_rows, rows), width), BF16), ((rows - q_rows, width), BF16)][:n_q]
    outs.append(((rows, 2 * width), BF16))
    *queries, kv = call(body, outs, [*flat, w3, col_sums])
    return queries, kv


def project_begin(chunks, steps, w3):
    n_here, n_chunk = len(chunks[0]), len(chunks)
    piece, _ = chunks[0][0].shape
    width = w3.shape[2]

    def body(*refs):
        w_ref, acc_ref, mom_ref = refs[n_here * n_chunk :]
        lane = lax.broadcasted_iota(jnp.int32, (piece, 128), 1)
        for c in range(n_chunk):
            blocks = refs[c * n_here : (c + 1) * n_here]
            at = pl.ds(c * piece, piece)
            for i in range(3):
                acc_ref[at, i * width : (i + 1) * width] = project_sum(
                    blocks, steps, w_ref, i
                )
            held = jnp.zeros((piece, 128), F32)
            for t, block in enumerate(blocks):
                for k, value in enumerate(moments(block[...])):
                    held = jnp.where(lane == 2 * t + k, value, held)
            mom_ref[at, :] = held

    flat = [b for chunk in chunks for b in chunk]
    outs = [((piece * n_chunk, 3 * width), F32), ((piece * n_chunk, 128), F32)]
    return call(body, outs, [*flat, w3])


def project_end(lasts, last, begun, w3, col_sums, kinds, ahead=()):
    n_chunk = len(lasts)
    piece, feats = lasts[0].shape
    width = w3.shape[2]
    skip = sum(a.shape[0] for a in ahead)
    rows = piece * n_chunk + skip
    n_begun = w3.shape[1] // feats - 1

    def body(*refs):
        w_ref, acc_ref, mom_ref, sum_ref, *ahead_refs, out_ref = refs[n_chunk:]
        for a in ahead_refs:
            out_ref[:skip, :] = a[...]
        for c in range(n_chunk):
            at = pl.ds(c * piece, piece)
            held = mom_ref[at, :]
            parts = [(held[:, 2 * t : 2 * t + 1], held[:, 2 * t + 1 : 2 * t + 2]) for t in range(n_begun)]
            parts.append(moments(refs[c][...]))
            mean, inv = joined_moments(parts, feats)
            for k, i in enumerate(kinds):
                cols = slice(i * width, (i + 1) * width)
                acc = acc_ref[at, cols] + project_sum([refs[c]], [last], w_ref, i)
                acc = (acc - mean * sum_ref[0:1, cols]) * inv
                to = pl.ds(skip + c * piece, piece)
                out_ref[to, k * width : (k + 1) * width] = acc.astype(BF16)

    outs = [((rows, len(kinds) * width), BF16)]
    return call(body, outs, [*lasts, w3, *begun, col_sums, *ahead])[0]


class Slots:
    def __init__(self, seg_len, early_rows):
        self.seg_len, self.early_rows = seg_len, early_rows
        self.offset = [(-a * seg_len) % RATE for a in range(RATE)]
        self.count = [(seg_len - o) // RATE for o in self.offset]
        self.tail = [seg_len - o - RATE * n for o, n in zip(self.offset, self.count)]
        self.early = [max(0, (early_rows - o) // RATE) for o in self.offset]
        self.late = [n - e for n, e in zip(self.count, self.early)]
        most = (
            max(e + o for e, o in zip(self.early, self.offset)),
            max(l + t for l, t in zip(self.late, self.tail)),
        )
        self.rows = [-(-m // 8) * 8 for m in most]
        self.pitch = [-(-m // 16) * 16 for m in most]
        self.joints = [b for b in range(RATE - 1) if self.tail[b] > 0]


def filter_rows(w_ref):
    return [
        jnp.concatenate([w_ref[r, k : k + 1, :].astype(F32) for k in range(2)], axis=1)
        for r in range(RATE)
    ]


def write_slots(slots, late, sources, w_ref, outs):
    weight = filter_rows(w_ref)
    n = slots.rows[late]
    main = sources[-1]
    base = slots.early_rows if late else 0
    counts = slots.late if late else slots.early
    begins = slots.early if late else [0] * RATE
    firsts = [slots.offset[a] + RATE * begins[a] for a in range(RATE)]
    wanted = sorted({f + r for f in firsts for r in range(RATE)})

    def hits(first, rows, at):
        row = lax.broadcasted_iota(jnp.int32, (n, rows), 0)
        col = lax.broadcasted_iota(jnp.int32, (n, rows), 1) + at
        return jnp.where(col == first + RATE * row, 1.0, 0.0)

    chosen = jnp.concatenate([hits(f, main.shape[0], base) for f in wanted], axis=0).astype(BF16)
    picks = jnp.dot(chosen, main[...], preferred_element_type=F32)
    row = lax.broadcasted_iota(jnp.int32, (n, 1), 0)
    picked = {}
    for k, f in enumerate(wanted):
        got = picks[k * n : (k + 1) * n]
        if f < base:
            back = base - f
            got = jnp.where(row == 0, sources[0][-16:, :].astype(F32)[16 - back : 17 - back], got)
        picked[f] = got
    raw = main[...].astype(F32)
    for a in range(RATE):
        acc = None
        for r in range(RATE):
            term = picked[firsts[a] + r] * weight[r]
            acc = term if acc is None else acc + term
        n_raw = slots.tail[a] if late else slots.offset[a]
        for i in range(n_raw):
            at = main.shape[0] - n_raw + i if late else i
            acc = jnp.where(row == counts[a] + i, raw[at : at + 1, :], acc)
        outs[a][...] = acc.astype(BF16)


def compress(slots, sources, weight):
    n_in = len(sources)

    def body(*refs):
        write_slots(slots, n_in == 2, refs[:n_in], refs[n_in], refs[n_in + 1 :])

    outs = [((slots.rows[n_in == 2], 2 * weight.shape[2]), BF16)] * RATE
    return call(body, outs, [*sources, weight])


SCALE = math.log2(math.e) / math.sqrt(DH)


def score(q, keys):
    return lax.dot_general(q, keys, (((1,), (1,)), ((), ())), preferred_element_type=F32)


def slot_bias(seg, n_cols, spans):
    col = lax.broadcasted_iota(jnp.int32, (1, n_cols), 1)
    valid = col < 0
    for begin, count in spans:
        valid |= (col >= begin) & (col < begin + count)
    return jnp.where(valid & (seg >= BACK), 0.0, NEG).astype(F32)


def attend_begin(slots, q, q_start, own, memory, early):
    rows, width = q.shape
    n, pitch = slots.rows[0], slots.pitch[0]
    n_comp = -(-RATE * pitch // 128) * 128
    heads = width // DH

    def body(q_ref, *refs):
        own_refs = refs[: len(own)]
        mem_ref = refs[len(own)]
        early_refs = refs[len(own) + 1 : len(own) + 1 + RATE]
        mix_ref, stat_ref, comp_ref = refs[len(own) + 1 + RATE :]
        seg = lax.axis_index("seg")
        comp_ref[...] = jnp.zeros((n_comp, 2 * width), BF16)
        for a in range(RATE):
            comp_ref[a * pitch : a * pitch + n, :] = early_refs[a][...]
        comp_bias = slot_bias(seg, n_comp, [(a * pitch, slots.early[a]) for a in range(RATE)])
        mem_bias = jnp.where(seg >= 1, 0.0, NEG).astype(F32)
        seen = []
        k_start = 0
        for o in own_refs:
            n_keys = min(o.shape[0], q_start + rows - k_start)
            mask = None
            if k_start + n_keys - 1 > q_start:
                q_row = lax.broadcasted_iota(jnp.int32, (rows, n_keys), 0) + q_start
                k_row = lax.broadcasted_iota(jnp.int32, (rows, n_keys), 1) + k_start
                mask = k_row <= q_row
            if n_keys > 0:
                seen.append((o, n_keys, mask))
            k_start += o.shape[0]
        lane = lax.broadcasted_iota(jnp.int32, (rows, 128), 1)
        stats = jnp.zeros((rows, 128), F32)
        for h in range(heads):
            kc = slice(h * DH, (h + 1) * DH)
            vc = slice(width + h * DH, width + (h + 1) * DH)
            q = q_ref[:, kc]
            pieces = [
                (score(q, comp_ref[:, kc]) + comp_bias, comp_ref, vc),
                (score(q, mem_ref[:, kc]) + mem_bias, mem_ref, vc),
            ]
            for o, n_keys, mask in seen:
                s = score(q, o[:n_keys, kc])
                pieces.append((s if mask is None else jnp.where(mask, s, NEG), o, vc))
            top, norm, mixed = gathered(pieces, None)
            mix_ref[:, kc] = mixed
            stats = jnp.where(lane == 2 * h, top, stats)
            stats = jnp.where(lane == 2 * h + 1, norm, stats)
        stat_ref[...] = stats

    outs = [((rows, width), F32), ((rows, 128), F32)]
    scratch = [pltpu.VMEM((n_comp, 2 * width), BF16)]
    return call(body, outs, [q, *own, memory, *early], scratch)


def gathered(pieces, so_far):
    top = None if so_far is None else so_far[0]
    for s, _, _ in pieces:
        m = jnp.max(s, axis=1, keepdims=True)
        top = m if top is None else jnp.maximum(top, m)
    norm = mixed = None
    if so_far is not None:
        shrink = jnp.exp2((so_far[0] - top) * SCALE)
        norm, mixed = so_far[1] * shrink, so_far[2] * shrink
    for s, v, cols in pieces:
        p = jnp.exp2((s - top) * SCALE)
        total = jnp.sum(p, axis=1, keepdims=True)
        part = jnp.dot(p.astype(BF16), v[: s.shape[1], cols], preferred_element_type=F32)
        norm = total if norm is None else norm + total
        mixed = part if mixed is None else mixed + part
    return top, norm, mixed


def state_of(mix_ref, stat_ref, h):
    top, norm = (stat_ref[:, 2 * h + k : 2 * h + k + 1] for k in range(2))
    return top, norm, mix_ref[:, h * DH : (h + 1) * DH]


def attend_more(q, begun, memory):
    rows, width = q.shape

    def body(q_ref, mix_ref, stat_ref, mem_ref, mix_out, stat_out):
        seg = lax.axis_index("seg")
        mem_bias = jnp.where(seg >= 1, 0.0, NEG).astype(F32)
        lane = lax.broadcasted_iota(jnp.int32, (rows, 128), 1)
        stats = jnp.zeros((rows, 128), F32)
        for h in range(width // DH):
            kc = slice(h * DH, (h + 1) * DH)
            vc = slice(width + h * DH, width + (h + 1) * DH)
            pieces = [(score(q_ref[:, kc], mem_ref[:, kc]) + mem_bias, mem_ref, vc)]
            top, norm, mixed = gathered(pieces, state_of(mix_ref, stat_ref, h))
            mix_out[:, kc] = mixed
            stats = jnp.where(lane == 2 * h, top, stats)
            stats = jnp.where(lane == 2 * h + 1, norm, stats)
        stat_out[...] = stats

    outs = [((rows, width), F32), ((rows, 128), F32)]
    return call(body, outs, [q, *begun, memory])


def attend_end(slots, q, begun, heads_of, late, weight):
    rows, width = q.shape
    n, pitch = slots.rows[1], slots.pitch[1]
    n_comp = -(-(RATE * pitch + 16) // 128) * 128
    heads = width // DH

    def body(q_ref, mix_ref, stat_ref, *refs):
        early_refs = refs[:RATE]
        late_refs = refs[RATE : 2 * RATE]
        w_ref, out_ref, comp_ref = refs[2 * RATE :]
        seg = lax.axis_index("seg")
        weight = filter_rows(w_ref)
        if n < pitch:
            comp_ref[: RATE * pitch, :] = jnp.zeros((RATE * pitch, 2 * width), BF16)
        for a in range(RATE):
            comp_ref[a * pitch : a * pitch + n, :] = late_refs[a][...]
        pad = n_comp - RATE * pitch
        row = lax.broadcasted_iota(jnp.int32, (pad, 1), 0)
        extra = jnp.zeros((pad, 2 * width), F32)
        for k, b in enumerate(slots.joints):
            at = slots.late[b]
            tail = late_refs[b][...].astype(F32)
            parts = [tail[at + i : at + i + 1] for i in range(slots.tail[b])]
            at = slots.early[b + 1]
            head = early_refs[b + 1][...].astype(F32)
            parts += [head[at + i : at + i + 1] for i in range(slots.offset[b + 1])]
            slot = sum(p * weight[r] for r, p in enumerate(parts))
            extra = jnp.where(row == k, slot, extra)
        comp_ref[RATE * pitch :, :] = extra.astype(BF16)
        spans = [(a * pitch, slots.late[a]) for a in range(RATE)]
        spans.append((RATE * pitch, len(slots.joints)))
        comp_bias = slot_bias(seg, n_comp, spans)
        for h in range(heads):
            kc = slice(h * DH, (h + 1) * DH)
            vc = slice(width + h * DH, width + (h + 1) * DH)
            pieces = [(score(q_ref[:, kc], comp_ref[:, kc]) + comp_bias, comp_ref, vc)]
            _, norm, mixed = gathered(pieces, state_of(mix_ref, stat_ref, h))
            out_ref[:, kc] = (mixed / norm).astype(BF16)

    outs = [((rows, width), BF16)]
    scratch = [pltpu.VMEM((n_comp, 2 * width), BF16)]
    args = [q, *begun, *heads_of, *late, weight]
    return call(body, outs, args, scratch)[0]


def output_begin(ctx, steps, w_full, xored):
    rows = ctx[0].shape[0]

    def body(*refs):
        w_ref, acc_ref = refs[len(ctx) :]
        acc_ref[...] = output_sum(refs[: len(ctx)], steps, w_ref, xored)

    outs = [((rows, w_full.shape[1]), F32)]
    return call(body, outs, [*ctx, w_full])[0]


def output_sum(ctx, steps, w_ref, xored):
    width = ctx[0].shape[1]
    unit = xored or width
    size = w_ref.shape[0] // width
    acc = None
    for t, c in zip(steps, ctx):
        for k in range(width // unit):
            block = source_of(t, size) * (width // unit) + k
            if xored:
                block = lax.bitwise_xor(block, lax.axis_index("seg"))
            start = pl.multiple_of(block * unit, unit)
            part = jnp.dot(
                c[:, k * unit : (k + 1) * unit],
                w_ref[pl.ds(start, unit), :],
                preferred_element_type=F32,
            )
            acc = part if acc is None else acc + part
    return acc


def output_end(offset, n_rows, last_step, ctx, begun, w_full, xored, result):
    rows = ctx.shape[0]
    columns = w_full.shape[1]
    n_extra = 1 if result is not None else 0
    n_copy = 4 if rows % 64 == 0 else 1
    part = rows // n_copy

    def body(ctx_ref, acc_ref, w_ref, *refs):
        out_ref, held, sems = refs[n_extra:]
        acc = output_sum([ctx_ref], [last_step], w_ref, xored)
        copies = []
        for k in range(n_copy):
            at = pl.ds(k * part, part)
            held[at, :] = (acc_ref[at, :] + acc[k * part : (k + 1) * part]).astype(BF16)
            to = out_ref.at[pl.ds(offset + k * part, part), :]
            copies.append(pltpu.make_async_copy(held.at[at, :], to, sems.at[k]))
            copies[-1].start()
        for copy in copies:
            copy.wait()

    args = [ctx, begun, w_full]
    in_specs = [vmem(), vmem(), vmem()]
    aliases = {}
    if result is not None:
        args.append(result)
        in_specs.append(hbm())
        aliases = {3: 0}
    return pl.pallas_call(
        body,
        out_shape=jax.ShapeDtypeStruct((n_rows, columns), BF16),
        in_specs=in_specs,
        out_specs=hbm(),
        scratch_shapes=[pltpu.VMEM((rows, columns), BF16), pltpu.SemaphoreType.DMA((n_copy,))],
        input_output_aliases=aliases,
        compiler_params=params(),
    )(*args)


def gather_rows(block, by_xor):
    size = lax.axis_size("seg")
    if size & (size - 1):
        return lax.all_gather(block, "seg", axis=0, tiled=True)
    seg = lax.axis_index("seg")
    step = 1
    while step < size:
        other = lax.ppermute(block, "seg", [(i, i ^ step) for i in range(size)])
        if by_xor:
            block = join(block, other)
        else:
            upper = (seg // step) % 2 == 1
            low = jnp.where(upper, other, block)
            high = jnp.where(upper, block, other)
            block = jnp.concatenate([low, high], axis=0)
        step *= 2
    return block


def local(layer_input, w_qkv, comp_weight, w_out):
    n_head = lax.axis_size("head")
    seg_len = layer_input.shape[1]
    rows = pltpu.with_memory_space_constraint(layer_input[0], pltpu.HBM)
    w3 = pltpu.with_memory_space_constraint(jnp.transpose(w_qkv, (1, 0, 2)), pltpu.HBM)
    width = w_qkv.shape[2]
    weight = comp_weight

    early_rows = seg_len * EARLY // 16
    early_piece, late_piece = early_rows // EARLY_PARTS, (seg_len - early_rows) // LATE_PARTS
    slots = Slots(seg_len, early_rows)
    starts = [c * early_piece for c in range(EARLY_PARTS)]
    first = [[chunk] for chunk in split(rows, starts, early_piece)]
    starts = [early_rows + c * late_piece for c in range(LATE_PARTS)]
    second = [[chunk] for chunk in split(rows, starts, late_piece)]
    n_seg = lax.axis_size("seg")
    own_rows = w_out.shape[0]
    power = n_seg & (n_seg - 1) == 0
    xored = own_rows if power and own_rows % DH == 0 and width % own_rows == 0 else 0

    w_vmem, col_sums = fetch_weights(w3)
    for t in range(1, n_head):
        for chunk in first:
            chunk.append(spread(chunk, t))
    w_full = gather_rows(w_out, xored)
    half = seg_len // 2
    queries, kv0 = project(first, w_vmem, col_sums, half)
    q0, ahead = queries[0], queries[1:]
    early_parts = compress(slots, [kv0], weight)
    mem0 = passed_along(kv0, 1)
    early = [passed_along(p, BACK - a) for a, p in enumerate(early_parts)]

    for t in range(1, n_head):
        for chunk in second:
            chunk.append(spread(chunk, t))
    final = min(FINAL, n_head - 1)
    steps = [t for t in range(n_head) if t != final]
    begun = project_begin([[chunk[t] for t in steps] for chunk in second], steps, w_vmem)
    lasts = [chunk[final] for chunk in second]
    kv1 = project_end(lasts, final, begun, w_vmem, col_sums, (1, 2))
    mem1 = passed_along(kv1, 1)
    late_parts = compress(slots, [kv0, kv1], weight)
    late = [passed_along(p, BACK - a) for a, p in enumerate(late_parts)]
    q1 = project_end(lasts, final, begun, w_vmem, col_sums, (0,), ahead)

    rings = []
    for h, (q, own) in enumerate(((q0, [kv0]), (q1, [kv0, kv1]))):
        part = attend_begin(slots, q, h * half, own, mem0, early)
        part = attend_more(q, part, mem1)
        ctx = attend_end(slots, q, part, early, late, weight)
        rings.append([ctx])
    for t in range(1, n_head):
        for ring in rings:
            ring.append(spread(ring, t))
    result = None
    for h, ring in enumerate(rings):
        part = output_begin([ring[t] for t in steps], steps, w_full, xored)
        result = output_end(h * half, seg_len, final, ring[final], part, w_full, xored, result)
    return result[None]


def solution(mesh):
    return jax.shard_map(
        local,
        mesh=mesh,
        in_specs=(
            P(None, "seg", "head"),
            P(None, None, "head"),
            P(None, None, "head"),
            P("seg", "head"),
        ),
        out_specs=P(None, "seg", "head"),
        check_vma=False,
    )
```
